256 devices in a mesh: rep: 32 (over y, z_hi, core), dom: 8 (over z_lo, x).
Axes of the slice: x: 4, y: 4, z: 8 (z_hi: 4, z_lo: 2; z = z_hi * 2 + z_lo), core: 2. Of those that a mesh axis runs over, the one named last changes fastest.
Arguments:
- atomic_locations: float32 [3, 32, 65536], P(None, 'rep', 'dom'), may hold values from -9 to 9
- atomic_speeds: float32 [3, 32, 65536], P(None, 'rep', 'dom'), may hold values from -6 to 6
- atomic_properties: float32 [3, 65536], P(None, 'dom'), as said below
- resident_tile_members: int32 [2, 32, 512], P(None, 'rep', 'dom'), may hold values from 0 to 63
- resident_tile_tally: int32 [32, 8], P('rep', 'dom'), may hold values from 1 to 64, as said below
- top_edge_groups: int32 [32, 256], P('rep', 'dom'), may hold values from 0 to 63, as said below
- bottom_edge_groups: int32 [32, 256], P('rep', 'dom'), may hold values from 0 to 63, as said below
- boundary_tile_slots: int32 [2, 32, 256], P(None, 'rep', 'dom'), may hold values from 0 to 31
- boundary_tile_tally: int32 [32, 8], P('rep', 'dom'), may hold values from 1 to 32, as said below
- spring_links: int32 [2, 32768], P(None, 'dom'), may hold values from 0 to 8191
- thermal_levels: float32 [32], replicated, may hold values from 1 to 4
- exchange_mate: int32 [32], replicated, may hold values from 0 to 31, as said below
Outputs:
- positions_out: float32 [3, 32, 65536], P(None, 'rep', 'dom')
- velocities_out: float32 [3, 32, 65536], P(None, 'rep', 'dom')
The draws below stay inside these ranges and needn't reach their ends.
Inputs may be any that keep to these rules, and one draw needn't show every extreme that they name: `resident_tile_tally`: the slots of one domain beyond its live count are padding. `boundary_tile_tally`: the slots of one domain beyond its live count are padding. `top_edge_groups`: the 32 entries of one domain are distinct clusters of that domain. `bottom_edge_groups`: the 32 entries of one domain are distinct clusters of that domain. exchange_mate[r] is r, r - 1 or r + 1, and exchange_mate[exchange_mate[r]] = r; the slot pairs 0, 1 and 30, 31 always swap. `atomic_properties`: row 0 charges, row 1 strengths between 0.5 and 1.5, row 2 inverse masses between 0.5 and 2.
All inputs are finite; a program needn't handle non-finite values.
Results may differ from the reference program's by a relative error of at most 0.0003.
Values sent between devices are 32-bit elements; how exact they have to be, the bound alone decides.
No kernel may reach another device: no remote copies, remote signals or barrier semaphores. Data moves between devices by JAX's collectives and lax.ppermute only.
A program may use at most 64 MiB of HBM per device.

```python
import math
import jax
import jax.numpy as jnp
from jax import lax

CL = 64
CA = 128
STEPS = 2
HC = 32
PL = 64
PI = 32
NB = 4096
THERMAL_COPIES = 32
DOMS = 8
ATOMS = 65536


def ragged_counts(key, largest):
    exponent = jax.random.randint(key, (THERMAL_COPIES, DOMS), 0, 4)
    counts = jnp.maximum(largest // jnp.left_shift(jnp.int32(1), exponent), 1)
    chosen_spot = jax.random.randint(jax.random.fold_in(key, 7), (), 0, THERMAL_COPIES * DOMS)
    counts = counts.reshape(-1).at[chosen_spot].set(largest)
    return counts.reshape(THERMAL_COPIES, DOMS).astype(jnp.int32)


def draw_resident_tile_tally(key, part):
    return ragged_counts(jax.random.fold_in(key, 11), PL)


def draw_boundary_tile_tally(key, part):
    return ragged_counts(jax.random.fold_in(key, 13), PI)


def facing_clusters(key):
    subkeys = jax.random.split(key, THERMAL_COPIES * DOMS)
    selected = jax.vmap(lambda subkey: jax.random.permutation(subkey, CL)[:HC])(subkeys)
    return selected.reshape(THERMAL_COPIES, DOMS * HC).astype(jnp.int32)


def draw_top_edge_groups(key, part):
    return facing_clusters(jax.random.fold_in(key, 17))


def draw_bottom_edge_groups(key, part):
    return facing_clusters(jax.random.fold_in(key, 19))


def draw_atomic_properties(key, part):
    first_key = jax.random.fold_in(key, 23)
    second_key = jax.random.fold_in(key, 29)
    third_key = jax.random.fold_in(key, 31)
    charge = jnp.clip(jax.random.normal(first_key, (ATOMS,), jnp.float32), -4.0, 4.0)
    strength = jax.random.uniform(second_key, (ATOMS,), jnp.float32, 0.5, 1.5)
    inv_mass = jnp.exp(jax.random.uniform(third_key, (ATOMS,), jnp.float32, jnp.log(0.5), jnp.log(2.0)))
    return jnp.stack([charge, strength, inv_mass]).astype(jnp.float32)


def draw_exchange_mate(key, part):
    phase = jax.random.randint(jax.random.fold_in(key, 37), (), 0, 2)
    accepted = jax.random.randint(jax.random.fold_in(key, 41), (THERMAL_COPIES,), 0, 2)
    slots = jnp.arange(THERMAL_COPIES, dtype=jnp.int32)
    last = THERMAL_COPIES - 1
    start = slots - (slots - 2 - phase) % 2
    usable = (start >= 2) & (start + 1 <= last - 2)
    taken = usable & (accepted[jnp.clip(start, 0, last)] == 1)
    mate = jnp.where(start == slots, slots + 1, slots - 1)
    inner = jnp.where(taken, mate, slots)
    edges = jnp.where(slots == 0, 1, jnp.where(slots == 1, 0, jnp.where(slots == last, last - 1, jnp.where(slots == last - 1, last, inner))))
    return edges.astype(jnp.int32)


def with_ends(values, stream_key, low, high):
    place = [jax.random.randint(jax.random.fold_in(stream_key, axis), (), 0, length) for axis, length in enumerate(values.shape)]
    widest = values.shape.index(max(values.shape))
    next_to = place[:widest] + [(place[widest] + 1) % values.shape[widest]] + place[widest + 1:]
    return values.at[tuple(place)].set(low).at[tuple(next_to)].set(high)


def block_scale(key, shape, cuts, least, high):
    def one(position, parts):
        steps = jax.random.uniform(jax.random.fold_in(jax.random.fold_in(key, 6), position), (parts,), jnp.float32, least / len(cuts), high / len(cuts))
        return jnp.repeat(jnp.exp(steps), shape[position] // parts).reshape((-1,) + (1,) * (len(shape) - position - 1))

    gain = one(*cuts[0])
    for cut in cuts[1:]:
        gain = gain * one(*cut)
    return gain


def scatter_about(rng, dims, scale, limit, shards=(), kind=jnp.bfloat16):
    loudness = block_scale(rng, dims, shards, -0.22, 0.18) if shards else 1.0
    array = jax.random.normal(rng, dims, jnp.float32) * scale * loudness
    return jnp.minimum(jnp.maximum(array, -limit), limit).astype(kind)


def setup_inputs(seed: int = 0) -> dict:
    splits = jax.random.split(jax.random.key(seed), 13)
    return {
        "atomic_locations": scatter_about(splits[0], (3, THERMAL_COPIES, ATOMS), 1.5, 9.0, ((1, 32), (2, 8)), jnp.float32),
        "atomic_speeds": scatter_about(splits[1], (3, THERMAL_COPIES, ATOMS), 1.0, 6.0, ((1, 32), (2, 8)), jnp.float32),
        "atomic_properties": draw_atomic_properties(jax.random.fold_in(splits[12], 71), 0),
        "resident_tile_members": with_ends(jax.random.randint(splits[3], (2, THERMAL_COPIES, DOMS * PL), 0, CL), jax.random.fold_in(splits[3], 1), 0, CL - 1).astype(jnp.int32),
        "resident_tile_tally": draw_resident_tile_tally(jax.random.fold_in(splits[12], 71), 0),
        "top_edge_groups": draw_top_edge_groups(jax.random.fold_in(splits[12], 71), 0),
        "bottom_edge_groups": draw_bottom_edge_groups(jax.random.fold_in(splits[12], 71), 0),
        "boundary_tile_slots": with_ends(jax.random.randint(splits[7], (2, THERMAL_COPIES, DOMS * PI), 0, HC), jax.random.fold_in(splits[7], 1), 0, HC - 1).astype(jnp.int32),
        "boundary_tile_tally": draw_boundary_tile_tally(jax.random.fold_in(splits[12], 71), 0),
        "spring_links": with_ends(jax.random.randint(splits[9], (2, DOMS * NB), 0, CL * CA), jax.random.fold_in(splits[9], 1), 0, (CL * CA) - 1).astype(jnp.int32),
        "thermal_levels": jnp.clip(jnp.exp(jax.random.uniform(splits[10], (THERMAL_COPIES,), jnp.float32, math.log(1.0), math.log(4.0))), 1.0, 4.0),
        "exchange_mate": draw_exchange_mate(jax.random.fold_in(splits[12], 71), 0),
    }


TIME_STEP = 0.05
WIDTH = 2.0
SOFTENING = 0.5
BOND_STIFFNESS = 1.0
BLOCK_LIMIT = 32

def block_forces(near_coords, far_coords, charge_near, charge_far, strength_near, strength_far):
    offset = near_coords[:, :, :, None] - far_coords[:, :, None, :]
    squared = lax.optimization_barrier(jnp.sum(offset * offset, axis=0))
    magnitude = 2.0 / WIDTH * (strength_near[:, :, None] * strength_far[:, None, :]) * jnp.exp(-squared / WIDTH) + charge_near[:, :, None] * charge_far[:, None, :] * (squared + SOFTENING) ** (-1.5)
    pair_push = magnitude[None] * offset
    return (lax.optimization_barrier(jnp.sum(pair_push, axis=3)), -lax.optimization_barrier(jnp.sum(pair_push, axis=2)))

def pair_forces(source, charge, strength, first_list, second_list, weight):
    total_pairs = first_list.shape[0]
    block_size = math.gcd(total_pairs, BLOCK_LIMIT)
    block_count = total_pairs // block_size
    entries = (first_list.reshape(block_count, block_size), second_list.reshape(block_count, block_size), weight.reshape(block_count, block_size))

    def accumulate(totals, block_entry):
        first_rows, second_rows, pair_weight = block_entry
        on_first, on_second = block_forces(source[:, first_rows], source[:, second_rows], charge[first_rows], charge[second_rows], strength[first_rows], strength[second_rows])
        totals = totals.at[:, first_rows].add(on_first * pair_weight[None, :, None])
        totals = totals.at[:, second_rows].add(on_second * pair_weight[None, :, None])
        return (totals, None)
    totals, unused = lax.scan(accumulate, jnp.zeros(source.shape, jnp.float32), entries)
    return totals

def bond_forces(flat, bond_first, bond_second):
    stretch = flat[:, bond_first] - flat[:, bond_second]
    result = jnp.zeros(flat.shape, jnp.float32)
    return result.at[:, bond_first].add(-BOND_STIFFNESS * stretch).at[:, bond_second].add(BOND_STIFFNESS * stretch)

def reference(atomic_locations, atomic_speeds, atomic_properties, resident_tile_members, resident_tile_tally, top_edge_groups, bottom_edge_groups, boundary_tile_slots, boundary_tile_tally, spring_links, thermal_levels, exchange_mate):
    charge = atomic_properties[0].reshape(DOMS * CL, CA)
    strength = atomic_properties[1].reshape(DOMS * CL, CA)
    inv_mass = atomic_properties[2].reshape(DOMS * CL, CA)
    block_base = jnp.arange(DOMS, dtype=jnp.int32) * CL
    upper = (jnp.arange(DOMS, dtype=jnp.int32) + 1) % DOMS
    bond_base = jnp.arange(spring_links.shape[1], dtype=jnp.int32) // NB * (CL * CA)
    bond_first = (spring_links[0] + bond_base).astype(jnp.int32)
    bond_second = (spring_links[1] + bond_base).astype(jnp.int32)

    def run_replica(entries):
        coords, speeds, lpairs, lcount, ups, downs, ipairs, icount = entries
        ups = ups.reshape(DOMS, HC)
        downs = downs.reshape(DOMS, HC)
        lpairs = lpairs.reshape(2, DOMS, PL)
        local_first = lpairs[0] + block_base[:, None]
        local_second = lpairs[1] + block_base[:, None]
        live_local = (jnp.arange(PL, dtype=jnp.int32)[None, :] < lcount[:, None]).astype(jnp.float32)
        local_weight = live_local * jnp.where(local_first == local_second, 0.5, 1.0).astype(jnp.float32)
        ipairs = ipairs.reshape(2, DOMS, PI)
        iface_first = jnp.take_along_axis(ups, ipairs[0], axis=1) + block_base[:, None]
        iface_second = jnp.take_along_axis(downs[upper], ipairs[1], axis=1) + block_base[upper][:, None]
        iface_weight = (jnp.arange(PI, dtype=jnp.int32)[None, :] < icount[:, None]).astype(jnp.float32)
        first_list = jnp.concatenate([local_first.reshape(-1), iface_first.reshape(-1)]).astype(jnp.int32)
        second_list = jnp.concatenate([local_second.reshape(-1), iface_second.reshape(-1)]).astype(jnp.int32)
        weight_all = jnp.concatenate([local_weight.reshape(-1), iface_weight.reshape(-1)])

        def total_force(current):
            pairs_part = pair_forces(current, charge, strength, first_list, second_list, weight_all)
            bonded = bond_forces(current.reshape(3, -1), bond_first, bond_second).reshape(current.shape)
            return pairs_part + bonded
        coords = coords.reshape(3, DOMS * CL, CA)
        speeds = speeds.reshape(3, DOMS * CL, CA)
        force = total_force(coords)
        for section in range(STEPS):
            speeds = speeds + 0.5 * TIME_STEP * inv_mass * force
            coords = coords + TIME_STEP * speeds
            force = total_force(coords)
            speeds = speeds + 0.5 * TIME_STEP * inv_mass * force
        return (coords.reshape(3, -1), speeds.reshape(3, -1))
    new_coords, new_speeds = lax.map(run_replica, (atomic_locations.transpose(1, 0, 2), atomic_speeds.transpose(1, 0, 2), resident_tile_members.transpose(1, 0, 2), resident_tile_tally, top_edge_groups, bottom_edge_groups, boundary_tile_slots.transpose(1, 0, 2), boundary_tile_tally))
    metropolis_probability = jnp.sqrt(thermal_levels / thermal_levels[exchange_mate])
    positions_out = new_coords[exchange_mate].transpose(1, 0, 2)
    velocities_out = (new_speeds[exchange_mate] * metropolis_probability[:, None, None]).transpose(1, 0, 2)
    return (positions_out, velocities_out)
```

```python
import functools
import math

import jax
import jax.numpy as jnp
from jax import lax
from jax.experimental import pallas as pl
from jax.experimental.pallas import tpu as pltpu
from jax.sharding import PartitionSpec as P

CA = 128
STEPS = 2
TIME_STEP = 0.05

F32 = jnp.float32
BF16 = jnp.bfloat16
LOG2E = 1.4426950408889634
GROUP = 16
BOND_CHUNK = 1024

SMEM = pl.BlockSpec(memory_space=pltpu.SMEM)
VMEM = pl.BlockSpec(memory_space=pltpu.VMEM)


def shifted(shard, axis, by):
    devices = lax.axis_size(axis)
    return lax.ppermute(shard, axis, [(i, (i + by) % devices) for i in range(devices)])


def swapped(shard, axis, start):
    devices = lax.axis_size(axis)
    pairs = []
    for i in range(start, devices - 1, 2):
        pairs += [(i, i + 1), (i + 1, i)]
    return lax.ppermute(shard, axis, pairs)


def split3(y):
    high = y.astype(BF16).astype(F32)
    rest = y - high
    middle = rest.astype(BF16).astype(F32)
    return high, middle, rest - middle


def near_features(x, y, z, rho):
    norm = x * x + y * y + z * z + 0.25
    one, zero = jnp.ones_like(x), jnp.zeros_like(x)
    rows = jnp.stack([-2.0 * x, -2.0 * y, -2.0 * z, one, norm, zero, rho, zero], axis=1)
    h, m, l = split3(rows)
    return jnp.concatenate([h, h, m, m, h, l, m, l], axis=1)


def far_features(x, y, z, rho):
    norm = x * x + y * y + z * z + 0.25
    one, zero = jnp.ones_like(x), jnp.zeros_like(x)
    h, m, l = split3(jnp.stack([x, y, z, norm, one, zero, zero, zero], axis=1))
    rh, rm, rl = split3(jnp.stack([zero] * 6 + [rho, zero], axis=1))
    space = jnp.concatenate([h, m, h, m, l, h, l, m], axis=1)
    ratio = jnp.concatenate([rh, rm, rh, rm, rl, rh, rl, rm], axis=1)
    return jnp.concatenate([space, ratio], axis=2).astype(BF16)


def moment_features(x, y, z, strength):
    g = strength * math.exp(0.25)
    zero = jnp.zeros_like(x)
    h, m, l = split3(jnp.stack([g * x, g * y, g * z, g, zero, zero, zero, zero], axis=1))
    return jnp.concatenate([h, m, l, jnp.zeros_like(h)], axis=1).astype(BF16)


def charge_ratio(charge, strength):
    return charge / strength * math.exp(-0.125)


def pair_scale(product):
    t = product[:, :CA]
    r = lax.rsqrt(t)
    c = jnp.exp2(t * (-0.5 * LOG2E)) + product[:, CA:] * (r * r * r)
    high = c.astype(BF16)
    return high, (c - high.astype(F32)).astype(BF16)


def folded(sums):
    sums = sums[:, :CA] + sums[:, CA:]
    return sums[0:8] + sums[8:16] + sums[16:24]


def bond_forces(bonds, x, out):
    half = x.shape[1] // 2
    high = x.astype(BF16).astype(F32)

    def lay(v):
        flat = (3 * half, CA)
        return jnp.concatenate([v[:, :half].reshape(flat), v[:, half:].reshape(flat)], axis=1)

    table = jnp.concatenate([lay(high), lay(x - high)], axis=0).astype(BF16)
    lane_id = lax.broadcasted_iota(jnp.int32, (2 * CA, BOND_CHUNK), 0).astype(F32).astype(BF16)
    row_id = lax.broadcasted_iota(jnp.int32, (half, BOND_CHUNK), 0)
    one, none = jnp.ones((), BF16), jnp.zeros((), BF16)
    out[...] = jnp.zeros_like(out)

    def chunk(k, carry):
        ends = []
        for e in range(2):
            atom = bonds[e : e + 1, pl.ds(k * BOND_CHUNK, BOND_CHUNK)]
            cluster = atom // CA
            lane = atom % CA + cluster // half * CA
            lane = jnp.broadcast_to(lane.astype(F32).astype(BF16), lane_id.shape)
            pick = jnp.where(lane_id == lane, one, none)
            mask = row_id == cluster % half
            rows = jnp.dot(table, pick, preferred_element_type=F32)
            rows = (rows[: 3 * half] + rows[3 * half :]).reshape(3, half, BOND_CHUNK)
            ends.append((pick, mask, jnp.sum(jnp.where(mask[None], rows, 0.0), axis=1)))
        pull = ends[1][2] - ends[0][2]
        pull_high = pull.astype(BF16).astype(F32)
        total = None
        for e in range(2):
            pick, mask, _ = ends[e]
            sign = 1.0 if e == 0 else -1.0
            spread = [
                jnp.where(mask, sign * part[c : c + 1], 0.0).astype(BF16)
                for part in (pull_high, pull - pull_high)
                for c in range(3)
            ]
            term = lax.dot_general(
                jnp.concatenate(spread, axis=0),
                pick,
                (((1,), (1,)), ((), ())),
                preferred_element_type=F32,
            )
            total = term if total is None else total + term
        out[...] += total
        return carry

    lax.fori_loop(0, bonds.shape[1] // BOND_CHUNK, chunk, 0)
    sums = out[...]
    sums = (sums[: 3 * half] + sums[3 * half :]).reshape(3, half, 2 * CA)
    return jnp.concatenate([sums[:, :, :CA], sums[:, :, CA:]], axis=1)


def local_kernel(pairs, tally, x_ref, props, bonds, acc, bonded, near, far, moments, bond_sums):
    clusters = x_ref.shape[1]
    x, y, z = x_ref[0], x_ref[1], x_ref[2]
    rho = charge_ratio(props[0], props[1])
    features = near_features(x, y, z, rho)
    for c in range(clusters):
        near[c] = jnp.transpose(features[c]).astype(BF16)
    far[...] = far_features(x, y, z, rho)
    moments[...] = moment_features(x, y, z, props[1])
    acc[...] = jnp.zeros_like(acc)
    live = tally[0, 0]

    def group(block, carry):
        slots = [block * GROUP + k for k in range(GROUP)]
        ends = [(pairs[0, s], pairs[1, s]) for s in slots]
        products = [jnp.dot(near[i], far[j], preferred_element_type=F32) for i, j in ends]
        scales = [pair_scale(p) for p in products]
        sums = []
        for (i, j), (high, low) in zip(ends, scales):
            on_far = jnp.dot(
                moments[i], jnp.concatenate([high, low], axis=1), preferred_element_type=F32
            )
            turned = jnp.concatenate([jnp.transpose(high), jnp.transpose(low)], axis=1)
            on_near = jnp.dot(moments[j], turned, preferred_element_type=F32)
            sums.append((folded(on_near), folded(on_far)))
        for s, (i, j), (on_near, on_far) in zip(slots, ends, sums):
            weight = jnp.where(s < live, jnp.where(i == j, 0.5, 1.0), 0.0)
            acc[i] += weight * on_near
            acc[j] += weight * on_far
        return carry

    lax.fori_loop(0, (live + GROUP - 1) // GROUP, group, 0)
    bonded[...] = bond_forces(bonds, x_ref[...], bond_sums)


def edge_kernel(
    last,
    kick,
    tops,
    bottoms,
    slots,
    tally,
    lower,
    x_ref,
    v_ref,
    props,
    acc_in,
    bonded,
    upper_x,
    upper_props,
    lower_x,
    lower_props,
    *rest,
):
    if last:
        v_out, near, far, moments, acc = rest
    else:
        x_out, v_out, to_upper, to_lower, near, far, moments, acc = rest
    clusters = x_ref.shape[1]
    facing = upper_x.shape[1]
    x, y, z = x_ref[0], x_ref[1], x_ref[2]
    far[...] = far_features(x, y, z, charge_ratio(props[0], props[1]))
    for side, (hx, hp) in enumerate(((upper_x, upper_props), (lower_x, lower_props))):
        features = near_features(hx[0], hx[1], hx[2], charge_ratio(hp[0], hp[1]))
        for c in range(facing):
            near[side * facing + c] = jnp.transpose(features[c]).astype(BF16)
        moments[pl.ds(side * facing, facing)] = moment_features(hx[0], hx[1], hx[2], hp[1])
    acc[...] = acc_in[...]

    def side_loop(live, target_of, source_of):
        def group(block, carry):
            ids = [block * GROUP + k for k in range(GROUP)]
            ends = [(target_of(s), source_of(s)) for s in ids]
            products = [jnp.dot(near[j], far[i], preferred_element_type=F32) for i, j in ends]
            scales = [pair_scale(p) for p in products]
            sums = [
                folded(
                    jnp.dot(moments[j], jnp.concatenate(scale, axis=1), preferred_element_type=F32)
                )
                for (i, j), scale in zip(ends, scales)
            ]
            for s, (i, j), total in zip(ids, ends, sums):
                acc[i] += jnp.where(s < live, 1.0, 0.0) * total
            return carry

        lax.fori_loop(0, (live + GROUP - 1) // GROUP, group, 0)

    width = slots.shape[1]
    side_loop(tally[0, 0], lambda s: tops[0, slots[0, s]], lambda s: slots[1, s])
    side_loop(
        lower[0, 2 * width],
        lambda s: bottoms[0, lower[0, width + s]],
        lambda s: facing + lower[0, s],
    )
    sums = acc[...]
    mass = kick * props[2]
    g = props[1]
    count = sums[:, 3, :]
    for c in range(3):
        force = g * (x_ref[c] * count - sums[:, c, :]) + bonded[c]
        v = v_ref[c] + mass * force
        v_out[c] = v
        if not last:
            x_out[c] = x_ref[c] + TIME_STEP * v
    if not last:
        pack_rows(tops, bottoms, x_out, to_upper, to_lower, 0)


def pack_rows(tops, bottoms, source, to_upper, to_lower, base):
    for k in range(to_upper.shape[1]):
        i, j = tops[0, k], bottoms[0, k]
        for c in range(source.shape[0]):
            to_upper[base + c, pl.ds(k, 1), :] = source[c, pl.ds(i, 1), :]
            to_lower[base + c, pl.ds(k, 1), :] = source[c, pl.ds(j, 1), :]


def pack_kernel(tops, bottoms, x_ref, props, to_upper, to_lower):
    pack_rows(tops, bottoms, x_ref, to_upper, to_lower, 0)
    pack_rows(tops, bottoms, props, to_upper, to_lower, 3)


def local(
    atomic_locations,
    atomic_speeds,
    atomic_properties,
    resident_tile_members,
    resident_tile_tally,
    top_edge_groups,
    bottom_edge_groups,
    boundary_tile_slots,
    boundary_tile_tally,
    spring_links,
    thermal_levels,
    exchange_mate,
):
    atoms = atomic_locations.shape[2]
    clusters = atoms // CA
    facing = top_edge_groups.shape[1]
    width = boundary_tile_slots.shape[2]
    shape = (3, clusters, CA)
    x = atomic_locations.reshape(shape)
    v = atomic_speeds.reshape(shape)
    props = atomic_properties.reshape(shape)
    pairs = resident_tile_members[:, 0]
    slots = boundary_tile_slots[:, 0]
    sds = jax.ShapeDtypeStruct

    index_row = jnp.concatenate(
        [slots[0], slots[1], boundary_tile_tally[0], jnp.zeros((CA - 2 * width - 1,), jnp.int32)]
    )[None]
    lower = shifted(index_row, "dom", 1)

    to_upper, to_lower = pl.pallas_call(
        pack_kernel,
        out_shape=(sds((6, facing, CA), F32),) * 2,
        in_specs=[SMEM] * 2 + [VMEM] * 2,
        out_specs=(VMEM,) * 2,
        name="pack",
    )(top_edge_groups, bottom_edge_groups, x, props)
    from_upper = shifted(to_lower, "dom", -1)
    from_lower = shifted(to_upper, "dom", 1)
    upper_x, upper_props = from_upper[:3], from_upper[3:]
    lower_x, lower_props = from_lower[:3], from_lower[3:]

    local_call = pl.pallas_call(
        local_kernel,
        out_shape=(sds((clusters, 8, CA), F32), sds(shape, F32)),
        in_specs=[SMEM] * 2 + [VMEM] * 3,
        out_specs=(VMEM,) * 2,
        scratch_shapes=[
            pltpu.VMEM((clusters, CA, 64), BF16),
            pltpu.VMEM((clusters, 64, 2 * CA), BF16),
            pltpu.VMEM((clusters, 32, CA), BF16),
            pltpu.VMEM((3 * clusters, 2 * CA), F32),
        ],
        cost_estimate=pl.CostEstimate(
            flops=2_000_000_000, bytes_accessed=1_000_000, transcendentals=2_000_000
        ),
        name="resident",
    )

    def edge_call(last, kick):
        return pl.pallas_call(
            functools.partial(edge_kernel, last, kick),
            out_shape=(sds(shape, F32),)
            if last
            else (sds(shape, F32),) * 2 + (sds((3, facing, CA), F32),) * 2,
            in_specs=[SMEM] * 5 + [VMEM] * 9,
            out_specs=(VMEM,) if last else (VMEM,) * 4,
            scratch_shapes=[
                pltpu.VMEM((2 * facing, CA, 64), BF16),
                pltpu.VMEM((clusters, 64, 2 * CA), BF16),
                pltpu.VMEM((2 * facing, 32, CA), BF16),
                pltpu.VMEM((clusters, 8, CA), F32),
            ],
            cost_estimate=pl.CostEstimate(
                flops=1_000_000_000, bytes_accessed=1_000_000, transcendentals=2_000_000
            ),
            name="edges",
        )

    for step in range(STEPS + 1):
        acc, bonded = local_call(pairs, resident_tile_tally, x, props, spring_links)
        last = step == STEPS
        kick = TIME_STEP * (0.5 if step == 0 or last else 1.0)
        results = edge_call(last, kick)(
            top_edge_groups,
            bottom_edge_groups,
            slots,
            boundary_tile_tally,
            lower,
            x,
            v,
            props,
            acc,
            bonded,
            upper_x,
            upper_props,
            lower_x,
            lower_props,
        )
        if last:
            (v,) = results
        else:
            x, v, to_upper, to_lower = results
            upper_x = shifted(to_lower, "dom", -1)
            lower_x = shifted(to_upper, "dom", 1)

    own = lax.axis_index("rep")
    mate = exchange_mate[own]
    ratio = jnp.sqrt(thermal_levels[own] / thermal_levels[mate])
    near_mate = own + 1 - 2 * (own % 2)

    def exchanged(state):
        one, two = swapped(state, "rep", 0), swapped(state, "rep", 1)
        return jnp.where(mate == own, state, jnp.where(mate == near_mate, one, two))

    out = (3, 1, atoms)
    return exchanged(x).reshape(out), (exchanged(v) * ratio).reshape(out)


def solution(mesh):
    placed = (
        P(None, "rep", "dom"),
        P(None, "rep", "dom"),
        P(None, "dom"),
        P(None, "rep", "dom"),
        P("rep", "dom"),
        P("rep", "dom"),
        P("rep", "dom"),
        P(None, "rep", "dom"),
        P("rep", "dom"),
        P(None, "dom"),
        P(),
        P(),
    )
    return jax.shard_map(
        local,
        mesh=mesh,
        in_specs=placed,
        out_specs=(P(None, "rep", "dom"), P(None, "rep", "dom")),
        check_vma=False,
    )
```

```python
import functools
import math

import jax
import jax.numpy as jnp
from jax import lax
from jax.experimental import pallas as pl
from jax.experimental.pallas import tpu as pltpu
from jax.sharding import PartitionSpec as P

CA = 128
STEPS = 2
TIME_STEP = 0.05

F32 = jnp.float32
BF16 = jnp.bfloat16
LOG2E = 1.4426950408889634
ROWS = 8
GROUP = 16
ROUNDS = 4
VMEM_LIMIT = 20 << 20

SMEM = pl.BlockSpec(memory_space=pltpu.SMEM)
VMEM = pl.BlockSpec(memory_space=pltpu.VMEM)


def shifted(shard, axis, by):
    devices = lax.axis_size(axis)
    return lax.ppermute(shard, axis, [(i, (i + by) % devices) for i in range(devices)])


def swapped(shard, axis, start):
    devices = lax.axis_size(axis)
    pairs = []
    for i in range(start, devices - 1, 2):
        pairs += [(i, i + 1), (i + 1, i)]
    return lax.ppermute(shard, axis, pairs)


def halves(a):
    high = a.astype(BF16).astype(F32)
    return high, (a - high).astype(BF16).astype(F32)


def tile(cluster):
    return pl.ds(pl.multiple_of(cluster * ROWS, ROWS), ROWS)


def stack_rows(stack, base, rows):
    for k, row in enumerate(rows):
        count = rows[0].shape[0]
        if not hasattr(row, "shape"):
            row = jnp.full((count, CA), row, F32)
        stack[pl.ds(base * ROWS + k, count, stride=ROWS), :] = row


def position_parts(x, y, z):
    (xh, xm), (yh, ym), (zh, zm) = halves(x), halves(y), halves(z)
    x, y, z = xh + xm, yh + ym, zh + zm
    norm = x * x + y * y + z * z + 0.25
    nh, nm = halves(norm)
    return (xh, yh, zh), (xm, ym, zm), (nh, nm, norm - nh - nm)


def near_stack(stacks, base, high, middle, norm, rho):
    rh, rm = rho
    stack_rows(stacks.at[0], base, [*high, norm[0], 1.0, 1.0, norm[2], rh])
    stack_rows(stacks.at[1], base, [*middle, norm[1], 0.0, 0.0, 0.0, rm])


def far_stack(stacks, high, middle, norm, rho):
    rh, rm = rho
    twice = [-2.0 * a for a in high]
    stack_rows(stacks.at[2], 0, [*twice, 1.0, norm[0], norm[2], 1.0, 0.0])
    stack_rows(stacks.at[3], 0, [*[-2.0 * a for a in middle], 0.0, norm[1], 0.0, 0.0, 0.0])
    zero = jnp.zeros_like(rh)
    stack_rows(stacks.at[4], 0, [zero] * 7 + [rh])
    stack_rows(stacks.at[5], 0, [zero] * 7 + [rm])


def moment_stack(stack, base, x, y, z, strength):
    g = strength * math.exp(0.25)
    parts = [halves(a) for a in (g * x, g * y, g * z, g)]
    stack_rows(stack, base, [p[0] for p in parts] + [p[1] for p in parts])


def fill_near(near, stacks, c):
    h, m = stacks[0, tile(c), :], stacks[1, tile(c), :]
    near[c] = jnp.transpose(jnp.concatenate([h, h, m, m], axis=0).astype(BF16))


def fill_far(far, stacks, c):
    h, m, rh, rm = [stacks[k, tile(c), :] for k in (2, 3, 4, 5)]
    space = jnp.concatenate([h, m], axis=0).astype(BF16)
    ratio = jnp.concatenate([rh, rm], axis=0).astype(BF16)
    far[c] = jnp.concatenate(
        [jnp.concatenate([space, space], axis=0), jnp.concatenate([ratio, ratio], axis=0)], axis=1
    )


def fill_moments(moments, stack, c):
    w = stack[tile(c), :]
    moments[c] = jnp.concatenate([w, jnp.zeros_like(w)], axis=0).astype(BF16)


def charge_ratio(charge, strength):
    return halves(charge / strength * math.exp(-0.125))


def pair_scale(product):
    t = product[:, :CA]
    r = lax.rsqrt(t)
    c = jnp.exp2(t * (-0.5 * LOG2E)) + product[:, CA:] * (r * r * r)
    high = c.astype(BF16)
    return high, (c - high.astype(F32)).astype(BF16)


def moment_sums(weights, scales):
    sums = jnp.dot(weights, scales, preferred_element_type=F32)[:ROWS]
    return sums[:, :CA] + sums[:, CA:]


def bond_table(x):
    half = x.shape[1] // 2
    high, low = halves(x)

    def lay(v):
        flat = (3 * half, CA)
        return jnp.concatenate([v[:, :half].reshape(flat), v[:, half:].reshape(flat)], axis=1)

    return jnp.concatenate([lay(high), lay(low)], axis=0).astype(BF16)


def bond_chunk(table, atoms):
    size = atoms.shape[1]
    half = table.shape[0] // 6
    lane_id = lax.broadcasted_iota(jnp.int32, (2 * CA, size), 0).astype(F32).astype(BF16)
    row_id = lax.broadcasted_iota(jnp.int32, (half, size), 0)
    one, none = jnp.ones((), BF16), jnp.zeros((), BF16)
    ends = []
    for e in range(2):
        atom = atoms[e : e + 1]
        cluster = atom // CA
        lane = (atom % CA + cluster // half * CA).astype(F32).astype(BF16)
        pick = jnp.where(lane_id == jnp.broadcast_to(lane, lane_id.shape), one, none)
        mask = row_id == cluster % half
        rows = jnp.dot(table, pick, preferred_element_type=F32)
        rows = (rows[: 3 * half] + rows[3 * half :]).reshape(3, half, size)
        ends.append((pick, mask, jnp.sum(jnp.where(mask[None], rows, 0.0), axis=1)))
    pull = ends[1][2] - ends[0][2]
    total = None
    for (pick, mask, _), sign in zip(ends, (1.0, -1.0)):
        spread = [
            jnp.where(mask, part[c : c + 1], 0.0).astype(BF16)
            for part in halves(sign * pull)
            for c in range(3)
        ]
        term = lax.dot_general(
            jnp.concatenate(spread, axis=0),
            pick,
            (((1,), (1,)), ((), ())),
            preferred_element_type=F32,
        )
        total = term if total is None else total + term
    return total


def local_kernel(
    pairs, tally, x_ref, props, bonds, acc, bonded, stacks, moment_rows, near, far, moments, table, bond_sums
):
    clusters = x_ref.shape[1]
    half = clusters // 2
    x, y, z = x_ref[0], x_ref[1], x_ref[2]
    parts = position_parts(x, y, z)
    rho = charge_ratio(props[0], props[1])
    near_stack(stacks, 0, *parts, rho)
    far_stack(stacks, *parts, rho)
    moment_stack(moment_rows, 0, x, y, z, props[1])
    for c in range(clusters):
        fill_near(near, stacks, c)
        fill_far(far, stacks, c)
        fill_moments(moments, moment_rows, c)
    acc[...] = jnp.zeros_like(acc)
    table[...] = bond_table(x_ref[...])
    bond_sums[...] = jnp.zeros_like(bond_sums)
    live = tally[0, 0]
    group = pairs.shape[1] // ROUNDS
    size = bonds.shape[1] // ROUNDS

    def round_of(block, carry):
        slots = [block * group + k for k in range(group)]
        ends = [(pairs[0, s], pairs[1, s]) for s in slots]
        products = [jnp.dot(near[i], far[j], preferred_element_type=F32) for i, j in ends]
        scales = [pair_scale(p) for p in products]
        sums = []
        for (i, j), (high, low) in zip(ends, scales):
            on_far = moment_sums(moments[i], jnp.concatenate([high, low], axis=1))
            turned = jnp.concatenate([jnp.transpose(high), jnp.transpose(low)], axis=1)
            sums.append((moment_sums(moments[j], turned), on_far))
        start = pl.multiple_of(block * size, size)
        bond_sums[...] += bond_chunk(table[...], bonds[:, pl.ds(start, size)])
        for s, (i, j), (on_near, on_far) in zip(slots, ends, sums):
            weight = jnp.where(s < live, jnp.where(i == j, 0.5, 1.0), 0.0)
            acc[tile(i), :] += weight * on_near
            acc[tile(j), :] += weight * on_far
        return carry

    lax.fori_loop(0, ROUNDS, round_of, 0)
    for c in range(3):
        both = bond_sums[pl.ds(c * half, half), :] + bond_sums[pl.ds((3 + c) * half, half), :]
        bonded[c, pl.ds(0, half), :] = both[:, :CA]
        bonded[c, pl.ds(half, half), :] = both[:, CA:]


def edge_kernel(
    last,
    kick,
    tops,
    bottoms,
    slots,
    tally,
    lower,
    x_ref,
    v_ref,
    props,
    acc_in,
    bonded,
    upper_x,
    lower_x,
    upper_start,
    lower_start,
    *rest,
):
    if last:
        v_out, stacks, moment_rows, near, far, moments, acc = rest
    else:
        x_out, v_out, to_upper, to_lower, stacks, moment_rows, near, far, moments, acc = rest
    clusters = x_ref.shape[1]
    facing = upper_x.shape[1]
    parts = position_parts(x_ref[0], x_ref[1], x_ref[2])
    far_stack(stacks, *parts, charge_ratio(props[0], props[1]))
    for side, (hx, hp) in enumerate(((upper_x, upper_start), (lower_x, lower_start))):
        rho = charge_ratio(hp[3], hp[4])
        near_stack(stacks, side * facing, *position_parts(hx[0], hx[1], hx[2]), rho)
        moment_stack(moment_rows, side * facing, hx[0], hx[1], hx[2], hp[4])
    for c in range(clusters):
        fill_far(far, stacks, c)
    for c in range(2 * facing):
        fill_near(near, stacks, c)
        fill_moments(moments, moment_rows, c)
    acc[...] = acc_in[...]

    def side_loop(live, target_of, source_of):
        def round_of(block, carry):
            ids = [block * GROUP + k for k in range(GROUP)]
            ends = [(target_of(s), source_of(s)) for s in ids]
            products = [jnp.dot(near[j], far[i], preferred_element_type=F32) for i, j in ends]
            scales = [pair_scale(p) for p in products]
            sums = [
                moment_sums(moments[j], jnp.concatenate(scale, axis=1))
                for (i, j), scale in zip(ends, scales)
            ]
            for s, (i, j), total in zip(ids, ends, sums):
                acc[tile(i), :] += jnp.where(s < live, 1.0, 0.0) * total
            return carry

        lax.fori_loop(0, (live + GROUP - 1) // GROUP, round_of, 0)

    width = slots.shape[1]
    side_loop(tally[0, 0], lambda s: tops[0, slots[0, s]], lambda s: slots[1, s])
    side_loop(
        lower[2, 0],
        lambda s: bottoms[0, lower[1, s]],
        lambda s: facing + lower[0, s],
    )

    def moment(k):
        high = acc[pl.ds(k, clusters, stride=ROWS), :]
        return high + acc[pl.ds(k + 4, clusters, stride=ROWS), :]

    mass = kick * props[2]
    g = props[1]
    count = moment(3)
    for c in range(3):
        force = g * (x_ref[c] * count - moment(c)) + bonded[c]
        v = v_ref[c] + mass * force
        v_out[c] = v
        if not last:
            x_out[c] = x_ref[c] + TIME_STEP * v
    if not last:
        pack_rows(tops, bottoms, x_out, to_upper, to_lower, 0, 3)


def pack_rows(tops, bottoms, source, to_upper, to_lower, base, count):
    for k in range(to_upper.shape[1]):
        i, j = tops[0, k], bottoms[0, k]
        up = [source[c, pl.ds(i, 1), :] for c in range(count)]
        down = [source[c, pl.ds(j, 1), :] for c in range(count)]
        for c in range(count):
            to_upper[base + c, pl.ds(k, 1), :] = up[c]
            to_lower[base + c, pl.ds(k, 1), :] = down[c]


def pack_kernel(
    tops, bottoms, levels, mates, x_ref, raw, slots, tally, props, to_upper, to_lower, index_rows, choice
):
    for c in range(3):
        for k in range(props.shape[1]):
            props[c, pl.ds(k, 1), :] = raw[pl.ds(c, 1), pl.ds(k * CA, CA)]
    pack_rows(tops, bottoms, x_ref, to_upper, to_lower, 0, 3)
    pack_rows(tops, bottoms, props, to_upper, to_lower, 3, 2)
    width = slots.shape[1]
    index_rows[...] = jnp.zeros_like(index_rows)
    index_rows[pl.ds(0, 2), pl.ds(0, width)] = slots[...]
    index_rows[pl.ds(2, 1), pl.ds(0, 1)] = tally[...]
    own = lax.axis_index("rep")
    mate = mates[own]
    near_mate = own + 1 - 2 * lax.rem(own, 2)
    row = (1, CA)
    ratio = jnp.full(row, levels[own], F32) / jnp.full(row, levels[mate], F32)
    choice[...] = jnp.zeros_like(choice)
    choice[pl.ds(0, 1), :] = jnp.full(row, jnp.where(mate == own, 1.0, 0.0), F32)
    choice[pl.ds(1, 1), :] = jnp.full(row, jnp.where(mate == near_mate, 1.0, 0.0), F32)
    choice[pl.ds(2, 1), :] = jnp.sqrt(ratio)


def local(
    atomic_locations,
    atomic_speeds,
    atomic_properties,
    resident_tile_members,
    resident_tile_tally,
    top_edge_groups,
    bottom_edge_groups,
    boundary_tile_slots,
    boundary_tile_tally,
    spring_links,
    thermal_levels,
    exchange_mate,
):
    atoms = atomic_locations.shape[2]
    clusters = atoms // CA
    facing = top_edge_groups.shape[1]
    shape = (3, clusters, CA)
    x = atomic_locations.reshape(shape)
    v = atomic_speeds.reshape(shape)
    pairs = resident_tile_members[:, 0]
    slots = boundary_tile_slots[:, 0]
    sds = jax.ShapeDtypeStruct
    params = pltpu.CompilerParams(vmem_limit_bytes=VMEM_LIMIT)

    props, to_upper, to_lower, index_rows, choice = pl.pallas_call(
        pack_kernel,
        out_shape=(
            sds(shape, F32),
            sds((5, facing, CA), F32),
            sds((5, facing, CA), F32),
            sds((ROWS, CA), jnp.int32),
            sds((ROWS, CA), F32),
        ),
        in_specs=[SMEM] * 4 + [VMEM] * 4,
        out_specs=(VMEM,) * 5,
        compiler_params=params,
        name="pack",
    )(
        top_edge_groups,
        bottom_edge_groups,
        thermal_levels,
        exchange_mate,
        x,
        atomic_properties,
        slots,
        boundary_tile_tally,
    )
    upper_start = shifted(to_lower, "dom", -1)
    lower_start = shifted(to_upper, "dom", 1)
    lower = shifted(index_rows, "dom", 1)

    def scratch(sources):
        return [
            pltpu.VMEM((6, clusters * ROWS, CA), F32),
            pltpu.VMEM((clusters * ROWS, CA), F32),
            pltpu.VMEM((sources, CA, 4 * ROWS), BF16),
            pltpu.VMEM((clusters, 4 * ROWS, 2 * CA), BF16),
            pltpu.VMEM((sources, 2 * ROWS, CA), BF16),
        ]

    local_call = pl.pallas_call(
        local_kernel,
        out_shape=(sds((clusters * ROWS, CA), F32), sds(shape, F32)),
        in_specs=[SMEM] * 2 + [VMEM] * 3,
        out_specs=(VMEM,) * 2,
        scratch_shapes=scratch(clusters)
        + [
            pltpu.VMEM((3 * clusters, 2 * CA), BF16),
            pltpu.VMEM((3 * clusters, 2 * CA), F32),
        ],
        compiler_params=params,
        cost_estimate=pl.CostEstimate(
            flops=2_000_000_000, bytes_accessed=1_000_000, transcendentals=2_000_000
        ),
        name="resident",
    )

    def edge_call(last, kick):
        return pl.pallas_call(
            functools.partial(edge_kernel, last, kick),
            out_shape=(sds(shape, F32),)
            if last
            else (sds(shape, F32),) * 2 + (sds((3, facing, CA), F32),) * 2,
            in_specs=[SMEM] * 5 + [VMEM] * 9,
            out_specs=(VMEM,) if last else (VMEM,) * 4,
            scratch_shapes=scratch(2 * facing) + [pltpu.VMEM((clusters * ROWS, CA), F32)],
            compiler_params=params,
            cost_estimate=pl.CostEstimate(
                flops=1_000_000_000, bytes_accessed=1_000_000, transcendentals=2_000_000
            ),
            name="edges",
        )

    upper_x, lower_x = upper_start, lower_start
    sent_x = None
    for step in range(STEPS + 1):
        acc, bonded = local_call(pairs, resident_tile_tally, x, props, spring_links)
        last = step == STEPS
        if last:
            sent_x, acc = lax.optimization_barrier((x, acc))
            swapped_x = swapped(sent_x, "rep", 0), swapped(sent_x, "rep", 1)
        kick = TIME_STEP * (0.5 if step == 0 or last else 1.0)
        results = edge_call(last, kick)(
            top_edge_groups,
            bottom_edge_groups,
            slots,
            boundary_tile_tally,
            lower,
            x,
            v,
            props,
            acc,
            bonded,
            upper_x,
            lower_x,
            upper_start,
            lower_start,
        )
        if last:
            (v,) = results
        else:
            x, v, to_upper, to_lower = results
            upper_x = shifted(to_lower, "dom", -1)
            lower_x = shifted(to_upper, "dom", 1)

    keep, near_mate, ratio = choice[0] > 0.5, choice[1] > 0.5, choice[2]

    def chosen(own, one, two):
        return jnp.where(keep, own, jnp.where(near_mate, one, two))

    out = (3, 1, atoms)
    swapped_v = swapped(v, "rep", 0), swapped(v, "rep", 1)
    return chosen(x, *swapped_x).reshape(out), (chosen(v, *swapped_v) * ratio).reshape(out)


def solution(mesh):
    placed = (
        P(None, "rep", "dom"),
        P(None, "rep", "dom"),
        P(None, "dom"),
        P(None, "rep", "dom"),
        P("rep", "dom"),
        P("rep", "dom"),
        P("rep", "dom"),
        P(None, "rep", "dom"),
        P("rep", "dom"),
        P(None, "dom"),
        P(),
        P(),
    )
    return jax.shard_map(
        local,
        mesh=mesh,
        in_specs=placed,
        out_specs=(P(None, "rep", "dom"), P(None, "rep", "dom")),
        check_vma=False,
    )
```

```python
import functools
import math

import jax
import jax.numpy as jnp
from jax import lax
from jax.experimental import pallas as pl
from jax.experimental.pallas import tpu as pltpu
from jax.sharding import PartitionSpec as P

CA = 128
STEPS = 2
TIME_STEP = 0.05

F32 = jnp.float32
BF16 = jnp.bfloat16
LOG2E = 1.4426950408889634
ROWS = 8
ROUNDS = 4
PIECES = 4
LAG_SCALE = 3
LAG_SUM = 6
EDGE_SCALE = 3
EDGE_SUM = 6
BOND_PULL = 2
BOND_SPREAD = 4
VMEM_LIMIT = 20 << 20

SMEM = pl.BlockSpec(memory_space=pltpu.SMEM)
VMEM = pl.BlockSpec(memory_space=pltpu.VMEM)


def shifted(shard, axis, by):
    devices = lax.axis_size(axis)
    return lax.ppermute(shard, axis, [(i, (i + by) % devices) for i in range(devices)])


def swapped(shard, axis, start):
    devices = lax.axis_size(axis)
    pairs = []
    for i in range(start, devices - 1, 2):
        pairs += [(i, i + 1), (i + 1, i)]
    return lax.ppermute(shard, axis, pairs)


def halves(a):
    high = a.astype(BF16).astype(F32)
    return high, (a - high).astype(BF16).astype(F32)


def tile(cluster):
    return pl.ds(pl.multiple_of(cluster * ROWS, ROWS), ROWS)


def stack_rows(stack, base, rows):
    for k, row in enumerate(rows):
        count = rows[0].shape[0]
        if not hasattr(row, "shape"):
            row = jnp.full((count, CA), row, F32)
        stack[pl.ds(base * ROWS + k, count, stride=ROWS), :] = row


def position_parts(x, y, z):
    (xh, xm), (yh, ym), (zh, zm) = halves(x), halves(y), halves(z)
    x, y, z = xh + xm, yh + ym, zh + zm
    norm = x * x + y * y + z * z + 0.25
    nh, nm = halves(norm)
    return (xh, yh, zh), (xm, ym, zm), (nh, nm, norm - nh - nm)


def near_stack(stacks, base, high, middle, norm):
    stack_rows(stacks.at[0], base, [*high, norm[0], 1.0, 1.0, norm[2], 0.0])
    stack_rows(stacks.at[1], base, [*middle, norm[1], 0.0, 0.0, 0.0, 0.0])


def far_stack(stacks, high, middle, norm):
    twice = [-2.0 * a for a in high]
    stack_rows(stacks.at[2], 0, [*twice, 1.0, norm[0], norm[2], 1.0, 0.0])
    stack_rows(stacks.at[3], 0, [*[-2.0 * a for a in middle], 0.0, norm[1], 0.0, 0.0, 0.0])


def fill_ratio(ratio, rho, base):
    for c in range(rho.shape[0]):
        ratio[base + c] = jnp.transpose(jnp.broadcast_to(rho[c : c + 1], (CA, CA)))


def moment_stack(stack, base, x, y, z, strength):
    g = strength * math.exp(0.25)
    parts = [halves(a) for a in (g * x, g * y, g * z, g)]
    stack_rows(stack, base, [p[0] for p in parts] + [p[1] for p in parts])


def both_orders(stacks, k, c):
    h, m = stacks[k, tile(c), :], stacks[k + 1, tile(c), :]
    return (
        jnp.concatenate([h, m], axis=0).astype(BF16),
        jnp.concatenate([m, h], axis=0).astype(BF16),
    )


def fill_near(near, stacks, c):
    near[c] = both_orders(stacks, 0, c)[0]


def fill_far(far, stacks, c):
    far[c, 0], far[c, 1] = both_orders(stacks, 2, c)


def fill_moments(moments, stack, c):
    w = stack[tile(c), :]
    moments[c] = jnp.concatenate([w, jnp.zeros_like(w)], axis=0).astype(BF16)


def distances(near, far, pair, other):
    left = [near[i] for i, _ in (pair, other)]
    left = jnp.transpose(jnp.concatenate([left[0], left[0], left[1], left[1]], axis=0))
    right = [jnp.concatenate([far[j, 0], far[j, 1]], axis=0) for _, j in (pair, other)]
    zero = jnp.zeros_like(right[0])
    right = jnp.concatenate(
        [
            jnp.concatenate([right[0], zero], axis=1),
            jnp.concatenate([zero, right[1]], axis=1),
        ],
        axis=0,
    )
    both = jnp.dot(left, right, preferred_element_type=F32)
    return both[:, :CA], both[:, CA:]


def charge_ratio(charge, strength):
    return charge / strength * math.exp(-0.125)


def pair_scale(t, near_rho, far_rho):
    r = lax.rsqrt(t)
    c = jnp.exp2(t * (-0.5 * LOG2E)) + (near_rho * far_rho) * (r * r * r)
    high = c.astype(BF16)
    return high, (c - high.astype(F32)).astype(BF16)


def moment_sums(weights, scales):
    sums = jnp.dot(weights, scales, preferred_element_type=F32)[:ROWS]
    return sums[:, :CA] + sums[:, CA:]


def split(a, parts):
    return halves(a) if parts == 2 else (a,)


def bond_table(x, parts):
    half = x.shape[1] // 2

    def lay(v):
        flat = (3 * half, CA)
        return jnp.concatenate([v[:, :half].reshape(flat), v[:, half:].reshape(flat)], axis=1)

    return jnp.concatenate([lay(part) for part in split(x, parts)], axis=0).astype(BF16)


def bond_picks(picks, masks, atoms, start):
    size = atoms.shape[1]
    half = masks.shape[1]
    lane_id = lax.broadcasted_iota(jnp.int32, (2 * CA, size), 0).astype(F32).astype(BF16)
    row_id = lax.broadcasted_iota(jnp.int32, (half, size), 0)
    one, none = jnp.ones((), BF16), jnp.zeros((), BF16)
    for e in range(2):
        atom = atoms[e : e + 1]
        cluster = atom // CA
        lane = (atom % CA + cluster // half * CA).astype(F32).astype(BF16)
        hit = lane_id == jnp.broadcast_to(lane, lane_id.shape)
        picks[e, :, pl.ds(start, size)] = jnp.where(hit, one, none)
        mask = jnp.where(row_id == cluster % half, 1.0, 0.0)
        masks[e, :, pl.ds(start, size)] = mask.astype(BF16)


def bond_gather(table, picks, start, size):
    return [
        jnp.dot(table, picks[e, :, pl.ds(start, size)], preferred_element_type=F32)
        for e in range(2)
    ]


def bond_pull(rows, masks, start, size):
    half = masks.shape[1]
    parts = rows[0].shape[0] // (3 * half)
    ends = []
    for e in range(2):
        mask = masks[e, :, pl.ds(start, size)].astype(F32)
        both = sum(rows[e][k * 3 * half : (k + 1) * 3 * half] for k in range(parts))
        ends.append(jnp.sum(both.reshape(3, half, size) * mask[None], axis=1))
    return split(ends[1] - ends[0], parts)


def bond_scatter(pull, picks, masks, start, size):
    half = masks.shape[1]
    total = None
    for e, sign in enumerate((1.0, -1.0)):
        mask = masks[e, :, pl.ds(start, size)]
        spread = [
            mask * jnp.broadcast_to(sign * part[c : c + 1], (half, size)).astype(BF16)
            for part in pull
            for c in range(3)
        ]
        term = lax.dot_general(
            jnp.concatenate(spread, axis=0),
            picks[e, :, pl.ds(start, size)],
            (((1,), (1,)), ((), ())),
            preferred_element_type=F32,
        )
        total = term if total is None else total + term
    return total


def pair_moments(moments, i, j, scale):
    high, low = scale
    on_far = moment_sums(moments[i], jnp.concatenate([high, low], axis=1))
    turned = jnp.concatenate([jnp.transpose(high), jnp.transpose(low)], axis=1)
    return moment_sums(moments[j], turned), on_far


def local_kernel(first, pairs, tally, x_ref, props, *rest):
    if first:
        bonds, acc, bonded, picks, masks, ratio, *scratch = rest
    else:
        x_before, bonded_before, picks, masks, ratio, acc, bonded, *scratch = rest
    stacks, moment_rows, near, far, moments, rho, table, bond_sums = scratch
    clusters = x_ref.shape[1]
    half = clusters // 2
    group = pairs.shape[1] // ROUNDS
    size = picks.shape[2] // ROUNDS
    x, y, z = x_ref[0], x_ref[1], x_ref[2]
    parts = position_parts(x, y, z)
    rho[...] = charge_ratio(props[0], props[1])
    if first:
        fill_ratio(ratio, rho[...], 0)
    near_stack(stacks, 0, *parts)
    far_stack(stacks, *parts)
    moment_stack(moment_rows, 0, x, y, z, props[1])
    for c in range(clusters):
        fill_near(near, stacks, c)
        fill_far(far, stacks, c)
        fill_moments(moments, moment_rows, c)
    acc[...] = jnp.zeros_like(acc)
    if first:
        table[...] = bond_table(x_ref[...], 2)
    else:
        table[...] = bond_table(x_ref[...] - x_before[...], 1)
    bond_sums[...] = jnp.zeros_like(bond_sums)
    live = tally[0, 0]

    def round_of(block, carry):
        start = pl.multiple_of(block * size, size)
        if first:
            bond_picks(picks, masks, bonds[:, pl.ds(start, size)], start)
        slots = [block * group + k for k in range(group)]
        ends = [(pairs[0, s], pairs[1, s]) for s in slots]
        piece = size // PIECES
        steps = group // PIECES
        products, scales, sums = [None] * group, [None] * group, [None] * group
        gathered, pulls, spread = [None] * PIECES, [None] * PIECES, None
        for t in range(group + LAG_SUM):
            if t < group and t % 2 == 0:
                products[t : t + 2] = distances(near, far, ends[t], ends[t + 1])
            q = t // steps
            if t % steps == 0 and q < PIECES:
                gathered[q] = bond_gather(table[...], picks, start + q * piece, piece)
            q = (t - BOND_PULL) // steps
            if (t - BOND_PULL) % steps == 0 and 0 <= q < PIECES:
                pulls[q] = bond_pull(gathered[q], masks, start + q * piece, piece)
            q = t - LAG_SCALE
            if 0 <= q < group:
                i, j = ends[q]
                scales[q] = pair_scale(products[q], ratio[i], rho[pl.ds(j, 1), :])
            q = t - LAG_SUM
            if 0 <= q < group:
                sums[q] = pair_moments(moments, *ends[q], scales[q])
            q = (t - BOND_SPREAD) // steps
            if (t - BOND_SPREAD) % steps == 0 and 0 <= q < PIECES:
                part = bond_scatter(pulls[q], picks, masks, start + q * piece, piece)
                spread = part if spread is None else spread + part
        bond_sums[...] += spread
        for s, (i, j), (on_near, on_far) in zip(slots, ends, sums):
            weight = jnp.where(s < live, jnp.where(i == j, 0.5, 1.0), 0.0)
            acc[tile(i), :] += weight * on_near
            acc[tile(j), :] += weight * on_far
        return carry

    lax.fori_loop(0, ROUNDS, round_of, 0)
    for c in range(3):
        both = bond_sums[pl.ds(c * half, half), :]
        if first:
            both = both + bond_sums[pl.ds((3 + c) * half, half), :]
        for k in range(2):
            new = both[:, k * CA : (k + 1) * CA]
            if not first:
                new = new + bonded_before[c, pl.ds(k * half, half), :]
            bonded[c, pl.ds(k * half, half), :] = new


def edge_kernel(
    first,
    last,
    kick,
    tops,
    bottoms,
    slots,
    tally,
    lower,
    x_ref,
    v_ref,
    props,
    acc_in,
    bonded,
    upper_x,
    lower_x,
    upper_start,
    lower_start,
    *rest,
):
    *rest, stacks, moment_rows, near, far, moments, rho, acc = rest
    if last:
        ratio, state = rest
    elif first:
        x_out, v_out, to_upper, to_lower, ratio = rest
    else:
        ratio, x_out, v_out, to_upper, to_lower = rest
    clusters = x_ref.shape[1]
    facing = upper_x.shape[1]
    parts = position_parts(x_ref[0], x_ref[1], x_ref[2])
    far_stack(stacks, *parts)
    rho[...] = charge_ratio(props[0], props[1])
    for side, (hx, hp) in enumerate(((upper_x, upper_start), (lower_x, lower_start))):
        if first:
            fill_ratio(ratio, charge_ratio(hp[3], hp[4]), side * facing)
        near_stack(stacks, side * facing, *position_parts(hx[0], hx[1], hx[2]))
        moment_stack(moment_rows, side * facing, hx[0], hx[1], hx[2], hp[4])
    for c in range(clusters):
        fill_far(far, stacks, c)
    for c in range(2 * facing):
        fill_near(near, stacks, c)
        fill_moments(moments, moment_rows, c)
    acc[...] = acc_in[...]

    width = slots.shape[1]
    ends, weights = [], []
    for s in range(width):
        ends.append((slots[1, s], tops[0, slots[0, s]]))
        weights.append(jnp.where(s < tally[0, 0], 1.0, 0.0))
        ends.append((facing + lower[0, s], bottoms[0, lower[1, s]]))
        weights.append(jnp.where(s < lower[2, 0], 1.0, 0.0))
    count = len(ends)
    products, scales = [None] * count, [None] * count
    for t in range(count + EDGE_SUM):
        if t < count and t % 2 == 0:
            products[t : t + 2] = distances(near, far, ends[t], ends[t + 1])
        q = t - EDGE_SCALE
        if 0 <= q < count:
            j, i = ends[q]
            scales[q] = pair_scale(products[q], ratio[j], rho[pl.ds(i, 1), :])
        q = t - EDGE_SUM
        if 0 <= q < count:
            j, i = ends[q]
            total = moment_sums(moments[j], jnp.concatenate(scales[q], axis=1))
            acc[tile(i), :] += weights[q] * total

    def moment(k):
        high = acc[pl.ds(k, clusters, stride=ROWS), :]
        return high + acc[pl.ds(k + 4, clusters, stride=ROWS), :]

    mass = kick * props[2]
    g = props[1]
    count = moment(3)
    for c in range(3):
        force = g * (x_ref[c] * count - moment(c)) + bonded[c]
        v = v_ref[c] + mass * force
        if last:
            state[c] = x_ref[c]
            state[3 + c] = v
        else:
            v_out[c] = v
            x_out[c] = x_ref[c] + TIME_STEP * v
    if not last:
        pack_rows(tops, bottoms, x_out, to_upper, to_lower, 0, 3)


def pack_rows(tops, bottoms, source, to_upper, to_lower, base, count):
    for k in range(to_upper.shape[1]):
        i, j = tops[0, k], bottoms[0, k]
        up = [source[c, pl.ds(i, 1), :] for c in range(count)]
        down = [source[c, pl.ds(j, 1), :] for c in range(count)]
        for c in range(count):
            to_upper[base + c, pl.ds(k, 1), :] = up[c]
            to_lower[base + c, pl.ds(k, 1), :] = down[c]


def pack_kernel(*refs):
    ins, outs, scratch, sems = refs[:8], refs[8:13], refs[13:21], refs[21]
    props, to_upper, to_lower, index_rows, choice = outs
    copies = [
        pltpu.make_async_copy(source, target, sems.at[k])
        for k, (source, target) in enumerate(zip(ins, scratch))
    ]
    for copy in copies:
        copy.start()
    for copy in copies:
        copy.wait()
    tops, bottoms, levels, mates, x_ref, raw, slots, tally = scratch
    for c in range(3):
        for k in range(props.shape[1]):
            props[c, pl.ds(k, 1), :] = raw[pl.ds(c, 1), pl.ds(k * CA, CA)]
    pack_rows(tops, bottoms, x_ref, to_upper, to_lower, 0, 3)
    pack_rows(tops, bottoms, props, to_upper, to_lower, 3, 2)
    width = slots.shape[1]
    index_rows[...] = jnp.zeros_like(index_rows)
    index_rows[pl.ds(0, 2), pl.ds(0, width)] = slots[...]
    index_rows[pl.ds(2, 1), pl.ds(0, 1)] = tally[...]
    own = lax.axis_index("rep")
    mate = mates[own]
    near_mate = own + 1 - 2 * lax.rem(own, 2)
    row = (1, CA)
    ratio = jnp.full(row, levels[own], F32) / jnp.full(row, levels[mate], F32)
    choice[...] = jnp.zeros_like(choice)
    choice[pl.ds(0, 1), :] = jnp.full(row, jnp.where(mate == own, 1.0, 0.0), F32)
    choice[pl.ds(1, 1), :] = jnp.full(row, jnp.where(mate == near_mate, 1.0, 0.0), F32)
    choice[pl.ds(2, 1), :] = jnp.sqrt(ratio)


def local(
    atomic_locations,
    atomic_speeds,
    atomic_properties,
    resident_tile_members,
    resident_tile_tally,
    top_edge_groups,
    bottom_edge_groups,
    boundary_tile_slots,
    boundary_tile_tally,
    spring_links,
    thermal_levels,
    exchange_mate,
):
    atoms = atomic_locations.shape[2]
    clusters = atoms // CA
    facing = top_edge_groups.shape[1]
    shape = (3, clusters, CA)
    x = atomic_locations.reshape(shape)
    v = atomic_speeds.reshape(shape)
    pairs = resident_tile_members[:, 0]
    slots = boundary_tile_slots[:, 0]
    sds = jax.ShapeDtypeStruct
    params = pltpu.CompilerParams(vmem_limit_bytes=VMEM_LIMIT)

    props, to_upper, to_lower, index_rows, choice = pl.pallas_call(
        pack_kernel,
        out_shape=(
            sds(shape, F32),
            sds((5, facing, CA), F32),
            sds((5, facing, CA), F32),
            sds((ROWS, CA), jnp.int32),
            sds((ROWS, CA), F32),
        ),
        in_specs=[pl.BlockSpec(memory_space=pltpu.HBM)] * 8,
        out_specs=(VMEM,) * 5,
        scratch_shapes=[
            pltpu.SMEM(top_edge_groups.shape, jnp.int32),
            pltpu.SMEM(bottom_edge_groups.shape, jnp.int32),
            pltpu.SMEM(thermal_levels.shape, F32),
            pltpu.SMEM(exchange_mate.shape, jnp.int32),
            pltpu.VMEM(shape, F32),
            pltpu.VMEM(atomic_properties.shape, F32),
            pltpu.VMEM(slots.shape, jnp.int32),
            pltpu.VMEM(boundary_tile_tally.shape, jnp.int32),
            pltpu.SemaphoreType.DMA((8,)),
        ],
        compiler_params=params,
        name="pack",
    )(
        top_edge_groups,
        bottom_edge_groups,
        thermal_levels,
        exchange_mate,
        x,
        atomic_properties,
        slots,
        boundary_tile_tally,
    )
    upper_start = shifted(to_lower, "dom", -1)
    lower_start = shifted(to_upper, "dom", 1)
    lower = shifted(index_rows, "dom", 1)

    def scratch(sources):
        return [
            pltpu.VMEM((4, clusters * ROWS, CA), F32),
            pltpu.VMEM((clusters * ROWS, CA), F32),
            pltpu.VMEM((sources, 2 * ROWS, CA), BF16),
            pltpu.VMEM((clusters, 2, 2 * ROWS, CA), BF16),
            pltpu.VMEM((sources, 2 * ROWS, CA), BF16),
            pltpu.VMEM((clusters, CA), F32),
        ]

    bonds = spring_links.shape[1]
    kept = (
        sds((2, 2 * CA, bonds), BF16),
        sds((2, clusters // 2, bonds), BF16),
        sds((clusters, CA, CA), F32),
    )

    def local_call(first):
        sums = (sds((clusters * ROWS, CA), F32), sds(shape, F32))
        rows = 3 * clusters if first else 3 * clusters // 2
        return pl.pallas_call(
            functools.partial(local_kernel, first),
            out_shape=sums + kept if first else sums,
            in_specs=[SMEM] * 2 + [VMEM] * (3 if first else 7),
            out_specs=(VMEM,) * (5 if first else 2),
            scratch_shapes=scratch(clusters)
            + [
                pltpu.VMEM((rows, 2 * CA), BF16),
                pltpu.VMEM((rows, 2 * CA), F32),
            ],
            compiler_params=params,
            cost_estimate=pl.CostEstimate(
                flops=2_000_000_000, bytes_accessed=1_000_000, transcendentals=2_000_000
            ),
            name="resident",
        )

    def edge_call(first, last, kick):
        if last:
            outs = (sds((6, clusters, CA), F32),)
        else:
            outs = (sds(shape, F32),) * 2 + (sds((3, facing, CA), F32),) * 2
        if first:
            outs += (sds((2 * facing, CA, CA), F32),)
        return pl.pallas_call(
            functools.partial(edge_kernel, first, last, kick),
            out_shape=outs,
            in_specs=[SMEM] * 5 + [VMEM] * (9 if first else 10),
            out_specs=(VMEM,) * len(outs),
            scratch_shapes=scratch(2 * facing) + [pltpu.VMEM((clusters * ROWS, CA), F32)],
            compiler_params=params,
            cost_estimate=pl.CostEstimate(
                flops=1_000_000_000, bytes_accessed=1_000_000, transcendentals=2_000_000
            ),
            name="edges",
        )

    halo_ratio = ()
    upper_x, lower_x = upper_start, lower_start
    for step in range(STEPS + 1):
        if step == 0:
            acc, bonded, *static = local_call(True)(
                pairs, resident_tile_tally, x, props, spring_links
            )
        else:
            acc, bonded = local_call(False)(
                pairs, resident_tile_tally, x, props, x_before, bonded, *static
            )
        last = step == STEPS
        kick = TIME_STEP * (0.5 if step == 0 or last else 1.0)
        results = edge_call(step == 0, last, kick)(
            top_edge_groups,
            bottom_edge_groups,
            slots,
            boundary_tile_tally,
            lower,
            x,
            v,
            props,
            acc,
            bonded,
            upper_x,
            lower_x,
            upper_start,
            lower_start,
            *halo_ratio,
        )
        if last:
            (state,) = results
        else:
            x_before = x
            x, v, to_upper, to_lower, *new_ratio = results
            halo_ratio = halo_ratio or new_ratio
            upper_x = shifted(to_lower, "dom", -1)
            lower_x = shifted(to_upper, "dom", 1)

    keep, near_mate, ratio = choice[0] > 0.5, choice[1] > 0.5, choice[2]

    def chosen(own, one, two):
        return jnp.where(keep, own, jnp.where(near_mate, one, two))

    out = (3, 1, atoms)
    new = chosen(state, swapped(state, "rep", 0), swapped(state, "rep", 1))
    return new[:3].reshape(out), (new[3:] * ratio).reshape(out)


def solution(mesh):
    placed = (
        P(None, "rep", "dom"),
        P(None, "rep", "dom"),
        P(None, "dom"),
        P(None, "rep", "dom"),
        P("rep", "dom"),
        P("rep", "dom"),
        P("rep", "dom"),
        P(None, "rep", "dom"),
        P("rep", "dom"),
        P(None, "dom"),
        P(),
        P(),
    )
    return jax.shard_map(
        local,
        mesh=mesh,
        in_specs=placed,
        out_specs=(P(None, "rep", "dom"), P(None, "rep", "dom")),
        check_vma=False,
    )
```

```python
import functools
import math

import jax
import jax.numpy as jnp
from jax import lax
from jax.experimental import pallas as pl
from jax.experimental.pallas import tpu as pltpu
from jax.sharding import PartitionSpec as P

CA = 128
STEPS = 2
TIME_STEP = 0.05

F32 = jnp.float32
BF16 = jnp.bfloat16
LOG2E = 1.4426950408889634
ROWS = 8
ROUNDS = 1
PIECES = 16
LAG_SCALE = 3
LAG_SUM = 6
EDGE_SCALE = 3
EDGE_SUM = 6
BOND_PULL = 2
BOND_SPREAD = 4
VMEM_LIMIT = 20 << 20
PACK_LIMIT = 60 << 20

SMEM = pl.BlockSpec(memory_space=pltpu.SMEM)
VMEM = pl.BlockSpec(memory_space=pltpu.VMEM)


def shifted(shard, axis, by):
    devices = lax.axis_size(axis)
    return lax.ppermute(shard, axis, [(i, (i + by) % devices) for i in range(devices)])


def swapped(shard, axis, start):
    devices = lax.axis_size(axis)
    pairs = []
    for i in range(start, devices - 1, 2):
        pairs += [(i, i + 1), (i + 1, i)]
    return lax.ppermute(shard, axis, pairs)


def halves(a):
    high = a.astype(BF16).astype(F32)
    return high, (a - high).astype(BF16).astype(F32)


def tile(cluster):
    return pl.ds(pl.multiple_of(cluster * ROWS, ROWS), ROWS)


def stack_rows(stack, base, rows):
    for k, row in enumerate(rows):
        count = rows[0].shape[0]
        if not hasattr(row, "shape"):
            row = jnp.full((count, CA), row, F32)
        stack[pl.ds(base * ROWS + k, count, stride=ROWS), :] = row


def position_parts(x, y, z):
    (xh, xm), (yh, ym), (zh, zm) = halves(x), halves(y), halves(z)
    x, y, z = xh + xm, yh + ym, zh + zm
    norm = x * x + y * y + z * z + 0.25
    nh, nm = halves(norm)
    return (xh, yh, zh), (xm, ym, zm), (nh, nm, norm - nh - nm)


def near_stack(stacks, base, high, middle, norm):
    stack_rows(stacks.at[0], base, [*high, norm[0], 1.0, 1.0, norm[2], 0.0])
    stack_rows(stacks.at[1], base, [*middle, norm[1], 0.0, 0.0, 0.0, 0.0])


def far_stack(stacks, high, middle, norm):
    twice = [-2.0 * a for a in high]
    stack_rows(stacks.at[2], 0, [*twice, 1.0, norm[0], norm[2], 1.0, 0.0])
    stack_rows(stacks.at[3], 0, [*[-2.0 * a for a in middle], 0.0, norm[1], 0.0, 0.0, 0.0])


def fill_ratio(ratio, rho, base):
    for c in range(rho.shape[0]):
        ratio[base + c] = jnp.transpose(jnp.broadcast_to(rho[c : c + 1], (CA, CA)))


def moment_stack(stack, base, x, y, z, strength):
    g = strength * math.exp(0.25)
    parts = [halves(a) for a in (g * x, g * y, g * z, g)]
    stack_rows(stack, base, [p[0] for p in parts] + [p[1] for p in parts])


def both_orders(stacks, k, c):
    h, m = stacks[k, tile(c), :], stacks[k + 1, tile(c), :]
    return (
        jnp.concatenate([h, m], axis=0).astype(BF16),
        jnp.concatenate([m, h], axis=0).astype(BF16),
    )


def fill_near(near, stacks, c):
    near[c] = both_orders(stacks, 0, c)[0]


def fill_far(far, stacks, c):
    far[c, 0], far[c, 1] = both_orders(stacks, 2, c)


def fill_moments(moments, stack, c):
    w = stack[tile(c), :]
    moments[c] = jnp.concatenate([w, jnp.zeros_like(w)], axis=0).astype(BF16)


def distances(near, far, pair, other):
    left = [near[i] for i, _ in (pair, other)]
    left = jnp.transpose(jnp.concatenate([left[0], left[0], left[1], left[1]], axis=0))
    right = [jnp.concatenate([far[j, 0], far[j, 1]], axis=0) for _, j in (pair, other)]
    zero = jnp.zeros_like(right[0])
    right = jnp.concatenate(
        [
            jnp.concatenate([right[0], zero], axis=1),
            jnp.concatenate([zero, right[1]], axis=1),
        ],
        axis=0,
    )
    both = jnp.dot(left, right, preferred_element_type=F32)
    return both[:, :CA], both[:, CA:]


def charge_ratio(charge, strength):
    return charge / strength * math.exp(-0.125)


def pair_scale(t, near_rho, far_rho):
    r = lax.rsqrt(t)
    c = jnp.exp2(t * (-0.5 * LOG2E)) + (near_rho * far_rho) * (r * r * r)
    high = c.astype(BF16)
    return high, (c - high.astype(F32)).astype(BF16)


def moment_sums(weights, scales):
    sums = jnp.dot(weights, scales, preferred_element_type=F32)[:ROWS]
    return sums[:, :CA] + sums[:, CA:]


def split(a, parts):
    return halves(a) if parts == 2 else (a,)


def bond_table(x, parts):
    half = x.shape[1] // 2

    def lay(v):
        flat = (3 * half, CA)
        return jnp.concatenate([v[:, :half].reshape(flat), v[:, half:].reshape(flat)], axis=1)

    return jnp.concatenate([lay(part) for part in split(x, parts)], axis=0).astype(BF16)


def bond_picks(picks, masks, atoms, start):
    size = atoms.shape[1]
    half = masks.shape[1]
    lane_id = lax.broadcasted_iota(jnp.int32, (2 * CA, size), 0).astype(F32).astype(BF16)
    row_id = lax.broadcasted_iota(jnp.int32, (half, size), 0)
    one, none = jnp.ones((), BF16), jnp.zeros((), BF16)
    for e in range(2):
        atom = atoms[e : e + 1]
        cluster = atom // CA
        lane = (atom % CA + cluster // half * CA).astype(F32).astype(BF16)
        hit = lane_id == jnp.broadcast_to(lane, lane_id.shape)
        picks[e, :, pl.ds(start, size)] = jnp.where(hit, one, none)
        mask = jnp.where(row_id == cluster % half, 1.0, 0.0)
        masks[e, :, pl.ds(start, size)] = mask.astype(BF16)


def bond_gather(table, picks, start, size):
    return [
        jnp.dot(table, picks[e, :, pl.ds(start, size)], preferred_element_type=F32)
        for e in range(2)
    ]


def bond_pull(rows, masks, start, size):
    half = masks.shape[1]
    parts = rows[0].shape[0] // (3 * half)
    ends = []
    for e in range(2):
        mask = masks[e, :, pl.ds(start, size)].astype(F32)
        both = sum(rows[e][k * 3 * half : (k + 1) * 3 * half] for k in range(parts))
        ends.append(jnp.sum(both.reshape(3, half, size) * mask[None], axis=1))
    return split(ends[1] - ends[0], parts)


def bond_scatter(pull, picks, masks, start, size):
    half = masks.shape[1]
    total = None
    for e, sign in enumerate((1.0, -1.0)):
        mask = masks[e, :, pl.ds(start, size)]
        spread = [
            mask * jnp.broadcast_to(sign * part[c : c + 1], (half, size)).astype(BF16)
            for part in pull
            for c in range(3)
        ]
        term = lax.dot_general(
            jnp.concatenate(spread, axis=0),
            picks[e, :, pl.ds(start, size)],
            (((1,), (1,)), ((), ())),
            preferred_element_type=F32,
        )
        total = term if total is None else total + term
    return total


def pair_moments(moments, i, j, scale):
    high, low = scale
    on_far = moment_sums(moments[i], jnp.concatenate([high, low], axis=1))
    turned = jnp.concatenate([jnp.transpose(high), jnp.transpose(low)], axis=1)
    return moment_sums(moments[j], turned), on_far


def local_kernel(first, pairs, tally, x_ref, props, *rest):
    if first:
        bonds, acc, bonded, picks, masks, ratio, *scratch = rest
    else:
        x_before, bonded_before, picks, masks, ratio, acc, bonded, *scratch = rest
    stacks, moment_rows, near, far, moments, rho, table, bond_sums = scratch
    clusters = x_ref.shape[1]
    half = clusters // 2
    group = pairs.shape[1] // ROUNDS
    size = picks.shape[2] // ROUNDS
    x, y, z = x_ref[0], x_ref[1], x_ref[2]
    parts = position_parts(x, y, z)
    rho[...] = charge_ratio(props[0], props[1])
    if first:
        fill_ratio(ratio, rho[...], 0)
    near_stack(stacks, 0, *parts)
    far_stack(stacks, *parts)
    moment_stack(moment_rows, 0, x, y, z, props[1])
    for c in range(clusters):
        fill_near(near, stacks, c)
        fill_far(far, stacks, c)
        fill_moments(moments, moment_rows, c)
    acc[...] = jnp.zeros_like(acc)
    if first:
        table[...] = bond_table(x_ref[...], 2)
    else:
        table[...] = bond_table(x_ref[...] - x_before[...], 1)
    bond_sums[...] = jnp.zeros_like(bond_sums)
    live = tally[0, 0]

    def round_of(block, carry):
        start = pl.multiple_of(block * size, size)
        if first:
            bond_picks(picks, masks, bonds[:, pl.ds(start, size)], start)
        slots = [block * group + k for k in range(group)]
        ends = [(pairs[0, s], pairs[1, s]) for s in slots]
        piece = size // PIECES
        steps = group // PIECES
        products, scales, sums = [None] * group, [None] * group, [None] * group
        gathered, pulls, spread = [None] * PIECES, [None] * PIECES, None
        for t in range(group + LAG_SUM):
            if t < group and t % 2 == 0:
                products[t : t + 2] = distances(near, far, ends[t], ends[t + 1])
            q = t // steps
            if t % steps == 0 and q < PIECES:
                gathered[q] = bond_gather(table[...], picks, start + q * piece, piece)
            q = (t - BOND_PULL) // steps
            if (t - BOND_PULL) % steps == 0 and 0 <= q < PIECES:
                pulls[q] = bond_pull(gathered[q], masks, start + q * piece, piece)
            q = t - LAG_SCALE
            if 0 <= q < group:
                i, j = ends[q]
                scales[q] = pair_scale(products[q], ratio[i], rho[pl.ds(j, 1), :])
            q = t - LAG_SUM
            if 0 <= q < group:
                sums[q] = pair_moments(moments, *ends[q], scales[q])
            q = (t - BOND_SPREAD) // steps
            if (t - BOND_SPREAD) % steps == 0 and 0 <= q < PIECES:
                part = bond_scatter(pulls[q], picks, masks, start + q * piece, piece)
                spread = part if spread is None else spread + part
        bond_sums[...] += spread
        for s, (i, j), (on_near, on_far) in zip(slots, ends, sums):
            weight = jnp.where(s < live, jnp.where(i == j, 0.5, 1.0), 0.0)
            acc[tile(i), :] += weight * on_near
            acc[tile(j), :] += weight * on_far
        return carry

    lax.fori_loop(0, ROUNDS, round_of, 0)
    for c in range(3):
        both = bond_sums[pl.ds(c * half, half), :]
        if first:
            both = both + bond_sums[pl.ds((3 + c) * half, half), :]
        for k in range(2):
            new = both[:, k * CA : (k + 1) * CA]
            if not first:
                new = new + bonded_before[c, pl.ds(k * half, half), :]
            bonded[c, pl.ds(k * half, half), :] = new


def edge_kernel(
    first,
    last,
    kick,
    tops,
    bottoms,
    slots,
    tally,
    lower,
    x_ref,
    v_ref,
    props,
    acc_in,
    bonded,
    upper_x,
    lower_x,
    upper_start,
    lower_start,
    *rest,
):
    *rest, stacks, moment_rows, near, far, moments, rho, acc = rest
    if last:
        ratio, state = rest
    elif first:
        x_out, v_out, to_upper, to_lower, ratio = rest
    else:
        ratio, x_out, v_out, to_upper, to_lower = rest
    clusters = x_ref.shape[1]
    facing = upper_x.shape[1]
    parts = position_parts(x_ref[0], x_ref[1], x_ref[2])
    far_stack(stacks, *parts)
    rho[...] = charge_ratio(props[0], props[1])
    for side, (hx, hp) in enumerate(((upper_x, upper_start), (lower_x, lower_start))):
        if first:
            fill_ratio(ratio, charge_ratio(hp[3], hp[4]), side * facing)
        near_stack(stacks, side * facing, *position_parts(hx[0], hx[1], hx[2]))
        moment_stack(moment_rows, side * facing, hx[0], hx[1], hx[2], hp[4])
    for c in range(clusters):
        fill_far(far, stacks, c)
    for c in range(2 * facing):
        fill_near(near, stacks, c)
        fill_moments(moments, moment_rows, c)
    acc[...] = acc_in[...]

    width = slots.shape[1]
    ends, weights = [], []
    for s in range(width):
        ends.append((slots[1, s], tops[0, slots[0, s]]))
        weights.append(jnp.where(s < tally[0, 0], 1.0, 0.0))
        ends.append((facing + lower[0, s], bottoms[0, lower[1, s]]))
        weights.append(jnp.where(s < lower[2, 0], 1.0, 0.0))
    count = len(ends)
    products, scales = [None] * count, [None] * count
    for t in range(count + EDGE_SUM):
        if t < count and t % 2 == 0:
            products[t : t + 2] = distances(near, far, ends[t], ends[t + 1])
        q = t - EDGE_SCALE
        if 0 <= q < count:
            j, i = ends[q]
            scales[q] = pair_scale(products[q], ratio[j], rho[pl.ds(i, 1), :])
        q = t - EDGE_SUM
        if 0 <= q < count:
            j, i = ends[q]
            total = moment_sums(moments[j], jnp.concatenate(scales[q], axis=1))
            acc[tile(i), :] += weights[q] * total

    def moment(k):
        high = acc[pl.ds(k, clusters, stride=ROWS), :]
        return high + acc[pl.ds(k + 4, clusters, stride=ROWS), :]

    mass = kick * props[2]
    g = props[1]
    count = moment(3)
    for c in range(3):
        force = g * (x_ref[c] * count - moment(c)) + bonded[c]
        v = v_ref[c] + mass * force
        if last:
            state[c] = x_ref[c]
            state[3 + c] = v
        else:
            v_out[c] = v
            x_out[c] = x_ref[c] + TIME_STEP * v
    if not last:
        pack_rows(tops, bottoms, x_out, to_upper, to_lower, 0, 3)


def pack_rows(tops, bottoms, source, to_upper, to_lower, base, count):
    for k in range(to_upper.shape[1]):
        i, j = tops[0, k], bottoms[0, k]
        up = [source[c, pl.ds(i, 1), :] for c in range(count)]
        down = [source[c, pl.ds(j, 1), :] for c in range(count)]
        for c in range(count):
            to_upper[base + c, pl.ds(k, 1), :] = up[c]
            to_lower[base + c, pl.ds(k, 1), :] = down[c]


def pack_kernel(
    tops, bottoms, levels, mates, x_ref, raw, slots, tally, props, to_upper, to_lower, index_rows, choice
):
    for c in range(3):
        for k in range(props.shape[1]):
            props[c, pl.ds(k, 1), :] = raw[pl.ds(c, 1), pl.ds(k * CA, CA)]
    pack_rows(tops, bottoms, x_ref, to_upper, to_lower, 0, 3)
    pack_rows(tops, bottoms, props, to_upper, to_lower, 3, 2)
    width = slots.shape[1]
    index_rows[...] = jnp.zeros_like(index_rows)
    index_rows[pl.ds(0, 2), pl.ds(0, width)] = slots[...]
    index_rows[pl.ds(2, 1), pl.ds(0, 1)] = tally[...]
    own = lax.axis_index("rep")
    mate = mates[own]
    near_mate = own + 1 - 2 * lax.rem(own, 2)
    row = (1, CA)
    ratio = jnp.full(row, levels[own], F32) / jnp.full(row, levels[mate], F32)
    choice[...] = jnp.zeros_like(choice)
    choice[pl.ds(0, 1), :] = jnp.full(row, jnp.where(mate == own, 1.0, 0.0), F32)
    choice[pl.ds(1, 1), :] = jnp.full(row, jnp.where(mate == near_mate, 1.0, 0.0), F32)
    choice[pl.ds(2, 1), :] = jnp.sqrt(ratio)


def local(
    atomic_locations,
    atomic_speeds,
    atomic_properties,
    resident_tile_members,
    resident_tile_tally,
    top_edge_groups,
    bottom_edge_groups,
    boundary_tile_slots,
    boundary_tile_tally,
    spring_links,
    thermal_levels,
    exchange_mate,
):
    atoms = atomic_locations.shape[2]
    clusters = atoms // CA
    facing = top_edge_groups.shape[1]
    shape = (3, clusters, CA)
    x = atomic_locations.reshape(shape)
    v = atomic_speeds.reshape(shape)
    pairs = resident_tile_members[:, 0]
    slots = boundary_tile_slots[:, 0]
    sds = jax.ShapeDtypeStruct
    params = pltpu.CompilerParams(vmem_limit_bytes=VMEM_LIMIT)

    props, to_upper, to_lower, index_rows, choice = pl.pallas_call(
        pack_kernel,
        out_shape=(
            sds(shape, F32),
            sds((5, facing, CA), F32),
            sds((5, facing, CA), F32),
            sds((ROWS, CA), jnp.int32),
            sds((ROWS, CA), F32),
        ),
        in_specs=[SMEM] * 4 + [VMEM] * 4,
        out_specs=(VMEM,) * 5,
        compiler_params=pltpu.CompilerParams(vmem_limit_bytes=PACK_LIMIT),
        name="pack",
    )(
        top_edge_groups,
        bottom_edge_groups,
        thermal_levels,
        exchange_mate,
        x,
        atomic_properties,
        slots,
        boundary_tile_tally,
    )
    upper_start = shifted(to_lower, "dom", -1)
    lower_start = shifted(to_upper, "dom", 1)
    lower = shifted(index_rows, "dom", 1)

    def scratch(sources):
        return [
            pltpu.VMEM((4, clusters * ROWS, CA), F32),
            pltpu.VMEM((clusters * ROWS, CA), F32),
            pltpu.VMEM((sources, 2 * ROWS, CA), BF16),
            pltpu.VMEM((clusters, 2, 2 * ROWS, CA), BF16),
            pltpu.VMEM((sources, 2 * ROWS, CA), BF16),
            pltpu.VMEM((clusters, CA), F32),
        ]

    bonds = spring_links.shape[1]
    kept = (
        sds((2, 2 * CA, bonds), BF16),
        sds((2, clusters // 2, bonds), BF16),
        sds((clusters, CA, CA), F32),
    )

    def local_call(first):
        sums = (sds((clusters * ROWS, CA), F32), sds(shape, F32))
        rows = 3 * clusters if first else 3 * clusters // 2
        return pl.pallas_call(
            functools.partial(local_kernel, first),
            out_shape=sums + kept if first else sums,
            in_specs=[SMEM] * 2 + [VMEM] * (3 if first else 7),
            out_specs=(VMEM,) * (5 if first else 2),
            scratch_shapes=scratch(clusters)
            + [
                pltpu.VMEM((rows, 2 * CA), BF16),
                pltpu.VMEM((rows, 2 * CA), F32),
            ],
            compiler_params=params,
            cost_estimate=pl.CostEstimate(
                flops=2_000_000_000, bytes_accessed=1_000_000, transcendentals=2_000_000
            ),
            name="resident",
        )

    def edge_call(first, last, kick):
        if last:
            outs = (sds((6, clusters, CA), F32),)
        else:
            outs = (sds(shape, F32),) * 2 + (sds((3, facing, CA), F32),) * 2
        if first:
            outs += (sds((2 * facing, CA, CA), F32),)
        return pl.pallas_call(
            functools.partial(edge_kernel, first, last, kick),
            out_shape=outs,
            in_specs=[SMEM] * 5 + [VMEM] * (9 if first else 10),
            out_specs=(VMEM,) * len(outs),
            scratch_shapes=scratch(2 * facing) + [pltpu.VMEM((clusters * ROWS, CA), F32)],
            compiler_params=params,
            cost_estimate=pl.CostEstimate(
                flops=1_000_000_000, bytes_accessed=1_000_000, transcendentals=2_000_000
            ),
            name="edges",
        )

    halo_ratio = ()
    upper_x, lower_x = upper_start, lower_start
    for step in range(STEPS + 1):
        if step == 0:
            acc, bonded, *static = local_call(True)(
                pairs, resident_tile_tally, x, props, spring_links
            )
        else:
            acc, bonded = local_call(False)(
                pairs, resident_tile_tally, x, props, x_before, bonded, *static
            )
        last = step == STEPS
        kick = TIME_STEP * (0.5 if step == 0 or last else 1.0)
        results = edge_call(step == 0, last, kick)(
            top_edge_groups,
            bottom_edge_groups,
            slots,
            boundary_tile_tally,
            lower,
            x,
            v,
            props,
            acc,
            bonded,
            upper_x,
            lower_x,
            upper_start,
            lower_start,
            *halo_ratio,
        )
        if last:
            (state,) = results
        else:
            x_before = x
            x, v, to_upper, to_lower, *new_ratio = results
            halo_ratio = halo_ratio or new_ratio
            upper_x = shifted(to_lower, "dom", -1)
            lower_x = shifted(to_upper, "dom", 1)

    keep, near_mate, ratio = choice[0] > 0.5, choice[1] > 0.5, choice[2]

    def chosen(own, one, two):
        return jnp.where(keep, own, jnp.where(near_mate, one, two))

    out = (3, 1, atoms)
    new = chosen(state, swapped(state, "rep", 0), swapped(state, "rep", 1))
    return new[:3].reshape(out), (new[3:] * ratio).reshape(out)


def solution(mesh):
    placed = (
        P(None, "rep", "dom"),
        P(None, "rep", "dom"),
        P(None, "dom"),
        P(None, "rep", "dom"),
        P("rep", "dom"),
        P("rep", "dom"),
        P("rep", "dom"),
        P(None, "rep", "dom"),
        P("rep", "dom"),
        P(None, "dom"),
        P(),
        P(),
    )
    return jax.shard_map(
        local,
        mesh=mesh,
        in_specs=placed,
        out_specs=(P(None, "rep", "dom"), P(None, "rep", "dom")),
        check_vma=False,
    )
```

```python
import functools
import math

import jax
import jax.numpy as jnp
from jax import lax
from jax.experimental import pallas as pl
from jax.experimental.pallas import tpu as pltpu
from jax.sharding import PartitionSpec as P

CA = 128
STEPS = 2
TIME_STEP = 0.05

F32 = jnp.float32
BF16 = jnp.bfloat16
LOG2E = 1.4426950408889634
ROWS = 8
ROUNDS = 1
PIECES = 16
LAG_SCALE = 3
LAG_SUM = 6
EDGE_SCALE = 3
EDGE_SUM = 6
BOND_PULL = 2
BOND_SPREAD = 4
VMEM_LIMIT = 20 << 20
PACK_LIMIT = 60 << 20
PACK_FLOPS = 2000

SMEM = pl.BlockSpec(memory_space=pltpu.SMEM)
VMEM = pl.BlockSpec(memory_space=pltpu.VMEM)


def swapped(shard, axis, start, ring=False):
    devices = lax.axis_size(axis)
    pairs = []
    for i in range(start, devices if ring else devices - 1, 2):
        other = (i + 1) % devices
        pairs += [(i, other), (other, i)]
    return lax.ppermute(shard, axis, pairs)


def side_lists(tops, bottoms):
    odd = lax.rem(lax.axis_index("dom"), 2) == 1

    def first(k):
        return jnp.where(odd, bottoms[0, k], tops[0, k])

    def second(k):
        return jnp.where(odd, tops[0, k], bottoms[0, k])

    return odd, first, second


def halves(a):
    high = a.astype(BF16).astype(F32)
    return high, (a - high).astype(BF16).astype(F32)


def tile(cluster):
    return pl.ds(pl.multiple_of(cluster * ROWS, ROWS), ROWS)


def stack_rows(stack, base, rows):
    for k, row in enumerate(rows):
        count = rows[0].shape[0]
        if not hasattr(row, "shape"):
            row = jnp.full((count, CA), row, F32)
        stack[pl.ds(base * ROWS + k, count, stride=ROWS), :] = row


def position_parts(x, y, z):
    (xh, xm), (yh, ym), (zh, zm) = halves(x), halves(y), halves(z)
    x, y, z = xh + xm, yh + ym, zh + zm
    norm = x * x + y * y + z * z + 0.25
    nh, nm = halves(norm)
    return (xh, yh, zh), (xm, ym, zm), (nh, nm, norm - nh - nm)


def near_stack(stacks, base, high, middle, norm):
    stack_rows(stacks.at[0], base, [*high, norm[0], 1.0, 1.0, norm[2], 0.0])
    stack_rows(stacks.at[1], base, [*middle, norm[1], 0.0, 0.0, 0.0, 0.0])


def far_stack(stacks, high, middle, norm):
    twice = [-2.0 * a for a in high]
    stack_rows(stacks.at[2], 0, [*twice, 1.0, norm[0], norm[2], 1.0, 0.0])
    stack_rows(stacks.at[3], 0, [*[-2.0 * a for a in middle], 0.0, norm[1], 0.0, 0.0, 0.0])


def fill_ratio(ratio, rho, base):
    for c in range(rho.shape[0]):
        ratio[base + c] = jnp.transpose(jnp.broadcast_to(rho[c : c + 1], (CA, CA)))


def moment_stack(stack, base, x, y, z, strength):
    g = strength * math.exp(0.25)
    parts = [halves(a) for a in (g * x, g * y, g * z, g)]
    stack_rows(stack, base, [p[0] for p in parts] + [p[1] for p in parts])


def both_orders(stacks, k, c):
    h, m = stacks[k, tile(c), :], stacks[k + 1, tile(c), :]
    return (
        jnp.concatenate([h, m], axis=0).astype(BF16),
        jnp.concatenate([m, h], axis=0).astype(BF16),
    )


def fill_near(near, stacks, c):
    near[c] = both_orders(stacks, 0, c)[0]


def fill_far(far, stacks, c):
    far[c, 0], far[c, 1] = both_orders(stacks, 2, c)


def fill_moments(moments, stack, c):
    w = stack[tile(c), :]
    moments[c] = jnp.concatenate([w, jnp.zeros_like(w)], axis=0).astype(BF16)


def distances(near, far, pair, other):
    left = [near[i] for i, _ in (pair, other)]
    left = jnp.transpose(jnp.concatenate([left[0], left[0], left[1], left[1]], axis=0))
    right = [jnp.concatenate([far[j, 0], far[j, 1]], axis=0) for _, j in (pair, other)]
    zero = jnp.zeros_like(right[0])
    right = jnp.concatenate(
        [
            jnp.concatenate([right[0], zero], axis=1),
            jnp.concatenate([zero, right[1]], axis=1),
        ],
        axis=0,
    )
    both = jnp.dot(left, right, preferred_element_type=F32)
    return both[:, :CA], both[:, CA:]


def charge_ratio(charge, strength):
    return charge / strength * math.exp(-0.125)


def pair_scale(t, near_rho, far_rho):
    r = lax.rsqrt(t)
    c = jnp.exp2(t * (-0.5 * LOG2E)) + (near_rho * far_rho) * (r * r * r)
    high = c.astype(BF16)
    return high, (c - high.astype(F32)).astype(BF16)


def moment_sums(weights, scales):
    sums = jnp.dot(weights, scales, preferred_element_type=F32)[:ROWS]
    return sums[:, :CA] + sums[:, CA:]


def split(a, parts):
    return halves(a) if parts == 2 else (a,)


def bond_table(x, parts):
    half = x.shape[1] // 2

    def lay(v):
        flat = (3 * half, CA)
        return jnp.concatenate([v[:, :half].reshape(flat), v[:, half:].reshape(flat)], axis=1)

    return jnp.concatenate([lay(part) for part in split(x, parts)], axis=0).astype(BF16)


def bond_picks(picks, masks, atoms, start):
    size = atoms.shape[1]
    half = masks.shape[1]
    lane_id = lax.broadcasted_iota(jnp.int32, (2 * CA, size), 0).astype(F32).astype(BF16)
    row_id = lax.broadcasted_iota(jnp.int32, (half, size), 0)
    one, none = jnp.ones((), BF16), jnp.zeros((), BF16)
    for e in range(2):
        atom = atoms[e : e + 1]
        cluster = atom // CA
        lane = (atom % CA + cluster // half * CA).astype(F32).astype(BF16)
        hit = lane_id == jnp.broadcast_to(lane, lane_id.shape)
        picks[e, :, pl.ds(start, size)] = jnp.where(hit, one, none)
        mask = jnp.where(row_id == cluster % half, 1.0, 0.0)
        masks[e, :, pl.ds(start, size)] = mask.astype(BF16)


def bond_gather(table, picks, start, size):
    return [
        jnp.dot(table, picks[e, :, pl.ds(start, size)], preferred_element_type=F32)
        for e in range(2)
    ]


def bond_pull(rows, masks, start, size):
    half = masks.shape[1]
    parts = rows[0].shape[0] // (3 * half)
    ends = []
    for e in range(2):
        mask = masks[e, :, pl.ds(start, size)].astype(F32)
        both = sum(rows[e][k * 3 * half : (k + 1) * 3 * half] for k in range(parts))
        ends.append(jnp.sum(both.reshape(3, half, size) * mask[None], axis=1))
    return split(ends[1] - ends[0], parts)


def bond_scatter(pull, picks, masks, start, size):
    half = masks.shape[1]
    total = None
    for e, sign in enumerate((1.0, -1.0)):
        mask = masks[e, :, pl.ds(start, size)]
        spread = [
            mask * jnp.broadcast_to(sign * part[c : c + 1], (half, size)).astype(BF16)
            for part in pull
            for c in range(3)
        ]
        term = lax.dot_general(
            jnp.concatenate(spread, axis=0),
            picks[e, :, pl.ds(start, size)],
            (((1,), (1,)), ((), ())),
            preferred_element_type=F32,
        )
        total = term if total is None else total + term
    return total


def pair_moments(moments, i, j, scale):
    high, low = scale
    on_far = moment_sums(moments[i], jnp.concatenate([high, low], axis=1))
    turned = jnp.concatenate([jnp.transpose(high), jnp.transpose(low)], axis=1)
    return moment_sums(moments[j], turned), on_far


def local_kernel(first, pairs, tally, x_ref, props, *rest):
    if first:
        raw = props
        bonds, acc, bonded, props, picks, masks, ratio, *scratch = rest
        relay_properties(raw, props)
    else:
        x_before, bonded_before, picks, masks, ratio, acc, bonded, *scratch = rest
    stacks, moment_rows, near, far, moments, rho, table, bond_sums = scratch
    clusters = x_ref.shape[1]
    half = clusters // 2
    group = pairs.shape[1] // ROUNDS
    size = picks.shape[2] // ROUNDS
    x, y, z = x_ref[0], x_ref[1], x_ref[2]
    parts = position_parts(x, y, z)
    rho[...] = charge_ratio(props[0], props[1])
    if first:
        fill_ratio(ratio, rho[...], 0)
    near_stack(stacks, 0, *parts)
    far_stack(stacks, *parts)
    moment_stack(moment_rows, 0, x, y, z, props[1])
    for c in range(clusters):
        fill_near(near, stacks, c)
        fill_far(far, stacks, c)
        fill_moments(moments, moment_rows, c)
    acc[...] = jnp.zeros_like(acc)
    if first:
        table[...] = bond_table(x_ref[...], 2)
    else:
        table[...] = bond_table(x_ref[...] - x_before[...], 1)
    bond_sums[...] = jnp.zeros_like(bond_sums)
    live = tally[0, 0]

    def round_of(block, carry):
        start = pl.multiple_of(block * size, size)
        if first:
            bond_picks(picks, masks, bonds[:, pl.ds(start, size)], start)
        slots = [block * group + k for k in range(group)]
        ends = [(pairs[0, s], pairs[1, s]) for s in slots]
        piece = size // PIECES
        steps = group // PIECES
        products, scales, sums = [None] * group, [None] * group, [None] * group
        gathered, pulls, spread = [None] * PIECES, [None] * PIECES, None
        for t in range(group + LAG_SUM):
            if t < group and t % 2 == 0:
                products[t : t + 2] = distances(near, far, ends[t], ends[t + 1])
            q = t // steps
            if t % steps == 0 and q < PIECES:
                gathered[q] = bond_gather(table[...], picks, start + q * piece, piece)
            q = (t - BOND_PULL) // steps
            if (t - BOND_PULL) % steps == 0 and 0 <= q < PIECES:
                pulls[q] = bond_pull(gathered[q], masks, start + q * piece, piece)
            q = t - LAG_SCALE
            if 0 <= q < group:
                i, j = ends[q]
                scales[q] = pair_scale(products[q], ratio[i], rho[pl.ds(j, 1), :])
            q = t - LAG_SUM
            if 0 <= q < group:
                sums[q] = pair_moments(moments, *ends[q], scales[q])
            q = (t - BOND_SPREAD) // steps
            if (t - BOND_SPREAD) % steps == 0 and 0 <= q < PIECES:
                part = bond_scatter(pulls[q], picks, masks, start + q * piece, piece)
                spread = part if spread is None else spread + part
        bond_sums[...] += spread
        for s, (i, j), (on_near, on_far) in zip(slots, ends, sums):
            weight = jnp.where(s < live, jnp.where(i == j, 0.5, 1.0), 0.0)
            acc[tile(i), :] += weight * on_near
            acc[tile(j), :] += weight * on_far
        return carry

    lax.fori_loop(0, ROUNDS, round_of, 0)
    for c in range(3):
        both = bond_sums[pl.ds(c * half, half), :]
        if first:
            both = both + bond_sums[pl.ds((3 + c) * half, half), :]
        for k in range(2):
            new = both[:, k * CA : (k + 1) * CA]
            if not first:
                new = new + bonded_before[c, pl.ds(k * half, half), :]
            bonded[c, pl.ds(k * half, half), :] = new


def edge_kernel(first, last, kick, tops, bottoms, slots, tally, *rest):
    if last:
        levels, mates, *rest = rest
    x_ref, v_ref, props, acc_in, bonded, first_x, second_x, first_start, second_start, *rest = rest
    *rest, stacks, moment_rows, near, far, moments, rho, acc, indices, lower, arrived = rest
    if last:
        ratio, state, choice = rest
        exchange_choice(levels, mates, choice)
    elif first:
        x_out, v_out, to_first, to_second, ratio = rest
    else:
        ratio, x_out, v_out, to_first, to_second = rest
    odd, _, _ = side_lists(tops, bottoms)
    rows = [start[5, pl.ds(0, ROWS), :] for start in (first_start, second_start)]
    indices[...] = jnp.where(odd, rows[0], rows[1]).astype(jnp.int32)
    fetch = pltpu.make_async_copy(indices, lower, arrived)
    fetch.start()
    clusters = x_ref.shape[1]
    facing = first_x.shape[1]
    parts = position_parts(x_ref[0], x_ref[1], x_ref[2])
    far_stack(stacks, *parts)
    rho[...] = charge_ratio(props[0], props[1])
    for side, (hx, hp) in enumerate(((first_x, first_start), (second_x, second_start))):
        if first:
            fill_ratio(ratio, charge_ratio(hp[3], hp[4]), side * facing)
        near_stack(stacks, side * facing, *position_parts(hx[0], hx[1], hx[2]))
        moment_stack(moment_rows, side * facing, hx[0], hx[1], hx[2], hp[4])
    for c in range(clusters):
        fill_far(far, stacks, c)
    for c in range(2 * facing):
        fill_near(near, stacks, c)
        fill_moments(moments, moment_rows, c)
    acc[...] = acc_in[...]

    width = slots.shape[1]
    upper_base = jnp.where(odd, facing, 0)
    lower_base = facing - upper_base
    fetch.wait()
    ends, weights = [], []
    for s in range(width):
        ends.append((upper_base + slots[1, s], tops[0, slots[0, s]]))
        weights.append(jnp.where(s < tally[0, 0], 1.0, 0.0))
        ends.append((lower_base + lower[0, s], bottoms[0, lower[1, s]]))
        weights.append(jnp.where(s < lower[2, 0], 1.0, 0.0))
    count = len(ends)
    products, scales = [None] * count, [None] * count
    for t in range(count + EDGE_SUM):
        if t < count and t % 2 == 0:
            products[t : t + 2] = distances(near, far, ends[t], ends[t + 1])
        q = t - EDGE_SCALE
        if 0 <= q < count:
            j, i = ends[q]
            scales[q] = pair_scale(products[q], ratio[j], rho[pl.ds(i, 1), :])
        q = t - EDGE_SUM
        if 0 <= q < count:
            j, i = ends[q]
            total = moment_sums(moments[j], jnp.concatenate(scales[q], axis=1))
            acc[tile(i), :] += weights[q] * total

    def moment(k):
        high = acc[pl.ds(k, clusters, stride=ROWS), :]
        return high + acc[pl.ds(k + 4, clusters, stride=ROWS), :]

    mass = kick * props[2]
    g = props[1]
    count = moment(3)
    for c in range(3):
        force = g * (x_ref[c] * count - moment(c)) + bonded[c]
        v = v_ref[c] + mass * force
        if last:
            state[c] = x_ref[c]
            state[3 + c] = v
        else:
            v_out[c] = v
            x_out[c] = x_ref[c] + TIME_STEP * v
    if not last:
        pack_rows(tops, bottoms, x_out, to_first, to_second, 0, 3)


def pack_rows(tops, bottoms, source, to_first, to_second, base, count):
    _, first, second = side_lists(tops, bottoms)
    for k in range(to_first.shape[1]):
        i, j = first(k), second(k)
        rows = [[source[c, pl.ds(n, 1), :] for c in range(count)] for n in (i, j)]
        for c in range(count):
            to_first[base + c, pl.ds(k, 1), :] = rows[0][c]
            to_second[base + c, pl.ds(k, 1), :] = rows[1][c]


def relay_properties(raw, props):
    for c in range(props.shape[0]):
        for k in range(props.shape[1]):
            props[c, pl.ds(k, 1), :] = raw[pl.ds(c, 1), pl.ds(k * CA, CA)]


def pack_kernel(tops, bottoms, x_ref, raw, slots, tally, to_first, to_second, props):
    relay_properties(raw, props)
    width = slots.shape[1]
    for buffer in (to_first, to_second):
        buffer[5] = jnp.zeros(buffer.shape[1:], F32)
        buffer[5, pl.ds(0, 2), pl.ds(0, width)] = slots[...].astype(F32)
        buffer[5, pl.ds(2, 1), pl.ds(0, 1)] = tally[...].astype(F32)
    pack_rows(tops, bottoms, x_ref, to_first, to_second, 0, 3)
    pack_rows(tops, bottoms, props, to_first, to_second, 3, 2)


def exchange_choice(levels, mates, choice):
    own = lax.axis_index("rep")
    mate = mates[own]
    near_mate = own + 1 - 2 * lax.rem(own, 2)
    row = (1, CA)
    ratio = jnp.full(row, levels[own], F32) / jnp.full(row, levels[mate], F32)
    choice[...] = jnp.zeros_like(choice)
    choice[pl.ds(0, 1), :] = jnp.full(row, jnp.where(mate == own, 1.0, 0.0), F32)
    choice[pl.ds(1, 1), :] = jnp.full(row, jnp.where(mate == near_mate, 1.0, 0.0), F32)
    choice[pl.ds(2, 1), :] = jnp.sqrt(ratio)


def local(
    atomic_locations,
    atomic_speeds,
    atomic_properties,
    resident_tile_members,
    resident_tile_tally,
    top_edge_groups,
    bottom_edge_groups,
    boundary_tile_slots,
    boundary_tile_tally,
    spring_links,
    thermal_levels,
    exchange_mate,
):
    atoms = atomic_locations.shape[2]
    clusters = atoms // CA
    facing = top_edge_groups.shape[1]
    shape = (3, clusters, CA)
    x = atomic_locations.reshape(shape)
    v = atomic_speeds.reshape(shape)
    pairs = resident_tile_members[:, 0]
    slots = boundary_tile_slots[:, 0]
    sds = jax.ShapeDtypeStruct
    params = pltpu.CompilerParams(vmem_limit_bytes=VMEM_LIMIT)

    to_first, to_second = pl.pallas_call(
        pack_kernel,
        out_shape=(sds((6, facing, CA), F32),) * 2,
        in_specs=[SMEM] * 2 + [VMEM] * 4,
        out_specs=(VMEM,) * 2,
        scratch_shapes=[pltpu.VMEM((2,) + shape[1:], F32)],
        compiler_params=pltpu.CompilerParams(vmem_limit_bytes=PACK_LIMIT),
        cost_estimate=pl.CostEstimate(
            flops=PACK_FLOPS * 1_000_000, bytes_accessed=1_000_000, transcendentals=0
        ),
        name="pack",
    )(
        top_edge_groups,
        bottom_edge_groups,
        x,
        atomic_properties,
        slots,
        boundary_tile_tally,
    )
    first_start = swapped(to_first, "dom", 0, True)
    second_start = swapped(to_second, "dom", 1, True)

    def scratch(sources):
        return [
            pltpu.VMEM((4, clusters * ROWS, CA), F32),
            pltpu.VMEM((clusters * ROWS, CA), F32),
            pltpu.VMEM((sources, 2 * ROWS, CA), BF16),
            pltpu.VMEM((clusters, 2, 2 * ROWS, CA), BF16),
            pltpu.VMEM((sources, 2 * ROWS, CA), BF16),
            pltpu.VMEM((clusters, CA), F32),
        ]

    bonds = spring_links.shape[1]
    kept = (
        sds(shape, F32),
        sds((2, 2 * CA, bonds), BF16),
        sds((2, clusters // 2, bonds), BF16),
        sds((clusters, CA, CA), F32),
    )

    def local_call(first):
        sums = (sds((clusters * ROWS, CA), F32), sds(shape, F32))
        rows = 3 * clusters if first else 3 * clusters // 2
        return pl.pallas_call(
            functools.partial(local_kernel, first),
            out_shape=sums + kept if first else sums,
            in_specs=[SMEM] * 2 + [VMEM] * (3 if first else 7),
            out_specs=(VMEM,) * (6 if first else 2),
            scratch_shapes=scratch(clusters)
            + [
                pltpu.VMEM((rows, 2 * CA), BF16),
                pltpu.VMEM((rows, 2 * CA), F32),
            ],
            compiler_params=params,
            cost_estimate=pl.CostEstimate(
                flops=2_000_000_000, bytes_accessed=1_000_000, transcendentals=2_000_000
            ),
            name="resident",
        )

    def edge_call(first, last, kick):
        if last:
            outs = (sds((6, clusters, CA), F32), sds((ROWS, CA), F32))
        else:
            outs = (sds(shape, F32),) * 2 + (sds((3, facing, CA), F32),) * 2
        if first:
            outs += (sds((2 * facing, CA, CA), F32),)
        return pl.pallas_call(
            functools.partial(edge_kernel, first, last, kick),
            out_shape=outs,
            in_specs=[SMEM] * (6 if last else 4) + [VMEM] * (9 if first else 10),
            out_specs=(VMEM,) * len(outs),
            scratch_shapes=scratch(2 * facing)
            + [
                pltpu.VMEM((clusters * ROWS, CA), F32),
                pltpu.VMEM((ROWS, CA), jnp.int32),
                pltpu.SMEM((ROWS, CA), jnp.int32),
                pltpu.SemaphoreType.DMA,
            ],
            compiler_params=params,
            cost_estimate=pl.CostEstimate(
                flops=1_000_000_000, bytes_accessed=1_000_000, transcendentals=2_000_000
            ),
            name="edges",
        )

    halo_ratio = ()
    first_x, second_x = first_start, second_start
    for step in range(STEPS + 1):
        if step == 0:
            acc, bonded, props, *static = local_call(True)(
                pairs, resident_tile_tally, x, atomic_properties, spring_links
            )
        else:
            acc, bonded = local_call(False)(
                pairs, resident_tile_tally, x, props, x_before, bonded, *static
            )
        last = step == STEPS
        kick = TIME_STEP * (0.5 if step == 0 or last else 1.0)
        results = edge_call(step == 0, last, kick)(
            top_edge_groups,
            bottom_edge_groups,
            slots,
            boundary_tile_tally,
            *((thermal_levels, exchange_mate) if last else ()),
            x,
            v,
            props,
            acc,
            bonded,
            first_x,
            second_x,
            first_start,
            second_start,
            *halo_ratio,
        )
        if last:
            state, choice = results
        else:
            x_before = x
            x, v, to_first, to_second, *new_ratio = results
            halo_ratio = halo_ratio or new_ratio
            first_x = swapped(to_first, "dom", 0, True)
            second_x = swapped(to_second, "dom", 1, True)

    keep, near_mate, ratio = choice[0] > 0.5, choice[1] > 0.5, choice[2]

    def chosen(own, one, two):
        return jnp.where(keep, own, jnp.where(near_mate, one, two))

    out = (3, 1, atoms)
    new = chosen(state, swapped(state, "rep", 0), swapped(state, "rep", 1))
    return new[:3].reshape(out), (new[3:] * ratio).reshape(out)


def solution(mesh):
    placed = (
        P(None, "rep", "dom"),
        P(None, "rep", "dom"),
        P(None, "dom"),
        P(None, "rep", "dom"),
        P("rep", "dom"),
        P("rep", "dom"),
        P("rep", "dom"),
        P(None, "rep", "dom"),
        P("rep", "dom"),
        P(None, "dom"),
        P(),
        P(),
    )
    return jax.shard_map(
        local,
        mesh=mesh,
        in_specs=placed,
        out_specs=(P(None, "rep", "dom"), P(None, "rep", "dom")),
        check_vma=False,
    )
```

```python
import functools
import math

import jax
import jax.numpy as jnp
from jax import lax
from jax.experimental import pallas as pl
from jax.experimental.pallas import tpu as pltpu
from jax.sharding import PartitionSpec as P

CA = 128
STEPS = 2
TIME_STEP = 0.05

F32 = jnp.float32
BF16 = jnp.bfloat16
LOG2E = 1.4426950408889634
ROWS = 8
ROUNDS = 1
PIECES = 16
LAG_SCALE = 3
LAG_SUM = 6
EDGE_SCALE = 3
EDGE_SUM = 6
BOND_PULL = 2
BOND_SPREAD = 4
VMEM_LIMIT = 20 << 20
PACK_LIMIT = 60 << 20
PACK_FLOPS = 2000

SMEM = pl.BlockSpec(memory_space=pltpu.SMEM)
VMEM = pl.BlockSpec(memory_space=pltpu.VMEM)


def swapped(shard, axis, start, ring=False):
    devices = lax.axis_size(axis)
    pairs = []
    for i in range(start, devices if ring else devices - 1, 2):
        other = (i + 1) % devices
        pairs += [(i, other), (other, i)]
    return lax.ppermute(shard, axis, pairs)


def side_lists(tops, bottoms):
    odd = lax.rem(lax.axis_index("dom"), 2) == 1

    def first(k):
        return jnp.where(odd, bottoms[0, k], tops[0, k])

    def second(k):
        return jnp.where(odd, tops[0, k], bottoms[0, k])

    return odd, first, second


def halves(a):
    high = a.astype(BF16).astype(F32)
    return high, (a - high).astype(BF16).astype(F32)


def tile(cluster):
    return pl.ds(pl.multiple_of(cluster * ROWS, ROWS), ROWS)


def stack_rows(stack, base, rows):
    for k, row in enumerate(rows):
        count = rows[0].shape[0]
        if not hasattr(row, "shape"):
            row = jnp.full((count, CA), row, F32)
        stack[pl.ds(base * ROWS + k, count, stride=ROWS), :] = row


def position_parts(x, y, z):
    (xh, xm), (yh, ym), (zh, zm) = halves(x), halves(y), halves(z)
    x, y, z = xh + xm, yh + ym, zh + zm
    norm = x * x + y * y + z * z + 0.25
    nh, nm = halves(norm)
    return (xh, yh, zh), (xm, ym, zm), (nh, nm, norm - nh - nm)


def near_stack(stacks, base, high, middle, norm):
    stack_rows(stacks.at[0], base, [*high, norm[0], 1.0, 1.0, norm[2], 0.0])
    stack_rows(stacks.at[1], base, [*middle, norm[1], 0.0, 0.0, 0.0, 0.0])


def far_stack(stacks, high, middle, norm):
    twice = [-2.0 * a for a in high]
    stack_rows(stacks.at[2], 0, [*twice, 1.0, norm[0], norm[2], 1.0, 0.0])
    stack_rows(stacks.at[3], 0, [*[-2.0 * a for a in middle], 0.0, norm[1], 0.0, 0.0, 0.0])


def fill_ratio(ratio, rho, base):
    for c in range(rho.shape[0]):
        ratio[base + c] = jnp.transpose(jnp.broadcast_to(rho[c : c + 1], (CA, CA)))


def moment_stack(stack, base, x, y, z, strength):
    g = strength * math.exp(0.25)
    parts = [halves(a) for a in (g * x, g * y, g * z, g)]
    stack_rows(stack, base, [p[0] for p in parts] + [p[1] for p in parts])


def both_orders(stacks, k, c):
    h, m = stacks[k, tile(c), :], stacks[k + 1, tile(c), :]
    return (
        jnp.concatenate([h, m], axis=0).astype(BF16),
        jnp.concatenate([m, h], axis=0).astype(BF16),
    )


def fill_near(near, stacks, c):
    near[c] = both_orders(stacks, 0, c)[0]


def fill_far(far, stacks, c):
    far[c, 0], far[c, 1] = both_orders(stacks, 2, c)


def fill_moments(moments, stack, c):
    w = stack[tile(c), :]
    moments[c] = jnp.concatenate([w, jnp.zeros_like(w)], axis=0).astype(BF16)


def distances(near, far, pair, other):
    left = [near[i] for i, _ in (pair, other)]
    left = jnp.transpose(jnp.concatenate([left[0], left[0], left[1], left[1]], axis=0))
    right = [jnp.concatenate([far[j, 0], far[j, 1]], axis=0) for _, j in (pair, other)]
    zero = jnp.zeros_like(right[0])
    right = jnp.concatenate(
        [
            jnp.concatenate([right[0], zero], axis=1),
            jnp.concatenate([zero, right[1]], axis=1),
        ],
        axis=0,
    )
    both = jnp.dot(left, right, preferred_element_type=F32)
    return both[:, :CA], both[:, CA:]


def charge_ratio(charge, strength):
    return charge / strength * math.exp(-0.125)


def pair_scale(t, near_rho, far_rho):
    r = lax.rsqrt(t)
    c = jnp.exp2(t * (-0.5 * LOG2E)) + (near_rho * far_rho) * (r * r * r)
    high = c.astype(BF16)
    return high, (c - high.astype(F32)).astype(BF16)


def moment_sums(weights, scales):
    sums = jnp.dot(weights, scales, preferred_element_type=F32)[:ROWS]
    return sums[:, :CA] + sums[:, CA:]


def split(a, parts):
    return halves(a) if parts == 2 else (a,)


def bond_table(x, parts):
    half = x.shape[1] // 2

    def lay(v):
        flat = (3 * half, CA)
        return jnp.concatenate([v[:, :half].reshape(flat), v[:, half:].reshape(flat)], axis=1)

    return jnp.concatenate([lay(part) for part in split(x, parts)], axis=0).astype(BF16)


def bond_picks(picks, masks, atoms, start):
    size = atoms.shape[1]
    half = masks.shape[1]
    lane_id = lax.broadcasted_iota(jnp.int32, (2 * CA, size), 0).astype(F32).astype(BF16)
    row_id = lax.broadcasted_iota(jnp.int32, (half, size), 0)
    one, none = jnp.ones((), BF16), jnp.zeros((), BF16)
    for e in range(2):
        atom = atoms[e : e + 1]
        cluster = atom // CA
        lane = (atom % CA + cluster // half * CA).astype(F32).astype(BF16)
        hit = lane_id == jnp.broadcast_to(lane, lane_id.shape)
        picks[e, :, pl.ds(start, size)] = jnp.where(hit, one, none)
        mask = jnp.where(row_id == cluster % half, 1.0, 0.0)
        masks[e, :, pl.ds(start, size)] = mask.astype(BF16)


def bond_gather(table, picks, start, size):
    return [
        jnp.dot(table, picks[e, :, pl.ds(start, size)], preferred_element_type=F32)
        for e in range(2)
    ]


def bond_pull(rows, masks, start, size):
    half = masks.shape[1]
    parts = rows[0].shape[0] // (3 * half)
    ends = []
    for e in range(2):
        mask = masks[e, :, pl.ds(start, size)].astype(F32)
        both = sum(rows[e][k * 3 * half : (k + 1) * 3 * half] for k in range(parts))
        ends.append(jnp.sum(both.reshape(3, half, size) * mask[None], axis=1))
    return split(ends[1] - ends[0], parts)


def bond_scatter(pull, picks, masks, start, size):
    half = masks.shape[1]
    total = None
    for e, sign in enumerate((1.0, -1.0)):
        mask = masks[e, :, pl.ds(start, size)]
        spread = [
            mask * jnp.broadcast_to(sign * part[c : c + 1], (half, size)).astype(BF16)
            for part in pull
            for c in range(3)
        ]
        term = lax.dot_general(
            jnp.concatenate(spread, axis=0),
            picks[e, :, pl.ds(start, size)],
            (((1,), (1,)), ((), ())),
            preferred_element_type=F32,
        )
        total = term if total is None else total + term
    return total


def pair_moments(moments, i, j, scale):
    high, low = scale
    on_far = moment_sums(moments[i], jnp.concatenate([high, low], axis=1))
    turned = jnp.concatenate([jnp.transpose(high), jnp.transpose(low)], axis=1)
    return moment_sums(moments[j], turned), on_far


def local_kernel(first, pairs, tally, x_ref, props, *rest):
    if first:
        raw = props
        bonds, acc, bonded, far, rho, props, picks, masks, ratio, *scratch = rest
        relay_properties(raw, props)
    else:
        x_before, bonded_before, picks, masks, ratio, acc, bonded, far, rho, *scratch = rest
    stacks, moment_rows, near, moments, table, bond_sums = scratch
    clusters = x_ref.shape[1]
    half = clusters // 2
    group = pairs.shape[1] // ROUNDS
    size = picks.shape[2] // ROUNDS
    x, y, z = x_ref[0], x_ref[1], x_ref[2]
    parts = position_parts(x, y, z)
    rho[...] = charge_ratio(props[0], props[1])
    if first:
        fill_ratio(ratio, rho[...], 0)
    near_stack(stacks, 0, *parts)
    far_stack(stacks, *parts)
    moment_stack(moment_rows, 0, x, y, z, props[1])
    for c in range(clusters):
        fill_near(near, stacks, c)
        fill_far(far, stacks, c)
        fill_moments(moments, moment_rows, c)
    acc[...] = jnp.zeros_like(acc)
    if first:
        table[...] = bond_table(x_ref[...], 2)
    else:
        table[...] = bond_table(x_ref[...] - x_before[...], 1)
    bond_sums[...] = jnp.zeros_like(bond_sums)
    live = tally[0, 0]

    def round_of(block, carry):
        start = pl.multiple_of(block * size, size)
        if first:
            bond_picks(picks, masks, bonds[:, pl.ds(start, size)], start)
        slots = [block * group + k for k in range(group)]
        ends = [(pairs[0, s], pairs[1, s]) for s in slots]
        piece = size // PIECES
        steps = group // PIECES
        products, scales, sums = [None] * group, [None] * group, [None] * group
        gathered, pulls, spread = [None] * PIECES, [None] * PIECES, None
        for t in range(group + LAG_SUM):
            if t < group and t % 2 == 0:
                products[t : t + 2] = distances(near, far, ends[t], ends[t + 1])
            q = t // steps
            if t % steps == 0 and q < PIECES:
                gathered[q] = bond_gather(table[...], picks, start + q * piece, piece)
            q = (t - BOND_PULL) // steps
            if (t - BOND_PULL) % steps == 0 and 0 <= q < PIECES:
                pulls[q] = bond_pull(gathered[q], masks, start + q * piece, piece)
            q = t - LAG_SCALE
            if 0 <= q < group:
                i, j = ends[q]
                scales[q] = pair_scale(products[q], ratio[i], rho[pl.ds(j, 1), :])
            q = t - LAG_SUM
            if 0 <= q < group:
                sums[q] = pair_moments(moments, *ends[q], scales[q])
            q = (t - BOND_SPREAD) // steps
            if (t - BOND_SPREAD) % steps == 0 and 0 <= q < PIECES:
                part = bond_scatter(pulls[q], picks, masks, start + q * piece, piece)
                spread = part if spread is None else spread + part
        bond_sums[...] += spread
        for s, (i, j), (on_near, on_far) in zip(slots, ends, sums):
            weight = jnp.where(s < live, jnp.where(i == j, 0.5, 1.0), 0.0)
            acc[tile(i), :] += weight * on_near
            acc[tile(j), :] += weight * on_far
        return carry

    lax.fori_loop(0, ROUNDS, round_of, 0)
    for c in range(3):
        both = bond_sums[pl.ds(c * half, half), :]
        if first:
            both = both + bond_sums[pl.ds((3 + c) * half, half), :]
        for k in range(2):
            new = both[:, k * CA : (k + 1) * CA]
            if not first:
                new = new + bonded_before[c, pl.ds(k * half, half), :]
            bonded[c, pl.ds(k * half, half), :] = new


def edge_kernel(first, last, kick, tops, bottoms, slots, tally, *rest):
    if first:
        mates, *rest = rest
    if last:
        levels, mates, *rest = rest
    x_ref, v_ref, props, acc_in, bonded, far, rho, *rest = rest
    first_x, second_x, first_start, second_start, *rest = rest
    *rest, stacks, moment_rows, near, moments, acc, indices, lower, arrived = rest
    if last:
        ratio, state, choice = rest
        exchange_choice(levels, mates, choice)
    elif first:
        x_out, v_out, to_first, to_second, ratio, crossing = rest
        across = jnp.int32(0)
        for r in range(mates.shape[0]):
            across = jnp.where((mates[r] != r) & (mates[r] != (r ^ 1)), 1, across)
        crossing[0, 0] = across
    else:
        ratio, x_out, v_out, to_first, to_second = rest
    odd, _, _ = side_lists(tops, bottoms)
    rows = [start[5, pl.ds(0, ROWS), :] for start in (first_start, second_start)]
    indices[...] = jnp.where(odd, rows[0], rows[1]).astype(jnp.int32)
    fetch = pltpu.make_async_copy(indices, lower, arrived)
    fetch.start()
    clusters = x_ref.shape[1]
    facing = first_x.shape[1]
    for side, (hx, hp) in enumerate(((first_x, first_start), (second_x, second_start))):
        if first:
            fill_ratio(ratio, charge_ratio(hp[3], hp[4]), side * facing)
        near_stack(stacks, side * facing, *position_parts(hx[0], hx[1], hx[2]))
        moment_stack(moment_rows, side * facing, hx[0], hx[1], hx[2], hp[4])
    for c in range(2 * facing):
        fill_near(near, stacks, c)
        fill_moments(moments, moment_rows, c)
    acc[...] = acc_in[...]

    width = slots.shape[1]
    upper_base = jnp.where(odd, facing, 0)
    lower_base = facing - upper_base
    fetch.wait()
    ends, weights = [], []
    for s in range(width):
        ends.append((upper_base + slots[1, s], tops[0, slots[0, s]]))
        weights.append(jnp.where(s < tally[0, 0], 1.0, 0.0))
        ends.append((lower_base + lower[0, s], bottoms[0, lower[1, s]]))
        weights.append(jnp.where(s < lower[2, 0], 1.0, 0.0))
    count = len(ends)
    products, scales = [None] * count, [None] * count
    for t in range(count + EDGE_SUM):
        if t < count and t % 2 == 0:
            products[t : t + 2] = distances(near, far, ends[t], ends[t + 1])
        q = t - EDGE_SCALE
        if 0 <= q < count:
            j, i = ends[q]
            scales[q] = pair_scale(products[q], ratio[j], rho[pl.ds(i, 1), :])
        q = t - EDGE_SUM
        if 0 <= q < count:
            j, i = ends[q]
            total = moment_sums(moments[j], jnp.concatenate(scales[q], axis=1))
            acc[tile(i), :] += weights[q] * total

    def moment(k):
        high = acc[pl.ds(k, clusters, stride=ROWS), :]
        return high + acc[pl.ds(k + 4, clusters, stride=ROWS), :]

    mass = kick * props[2]
    g = props[1]
    count = moment(3)
    for c in range(3):
        force = g * (x_ref[c] * count - moment(c)) + bonded[c]
        v = v_ref[c] + mass * force
        if last:
            state[c] = x_ref[c]
            state[3 + c] = v
        else:
            v_out[c] = v
            x_out[c] = x_ref[c] + TIME_STEP * v
    if not last:
        pack_rows(tops, bottoms, x_out, to_first, to_second, 0, 3)


def pack_rows(tops, bottoms, source, to_first, to_second, base, count):
    _, first, second = side_lists(tops, bottoms)
    for k in range(to_first.shape[1]):
        i, j = first(k), second(k)
        rows = [[source[c, pl.ds(n, 1), :] for c in range(count)] for n in (i, j)]
        for c in range(count):
            to_first[base + c, pl.ds(k, 1), :] = rows[0][c]
            to_second[base + c, pl.ds(k, 1), :] = rows[1][c]


def relay_properties(raw, props):
    for c in range(props.shape[0]):
        for k in range(props.shape[1]):
            props[c, pl.ds(k, 1), :] = raw[pl.ds(c, 1), pl.ds(k * CA, CA)]


def pack_kernel(tops, bottoms, x_ref, raw, slots, tally, to_first, to_second, props):
    relay_properties(raw, props)
    width = slots.shape[1]
    for buffer in (to_first, to_second):
        buffer[5] = jnp.zeros(buffer.shape[1:], F32)
        buffer[5, pl.ds(0, 2), pl.ds(0, width)] = slots[...].astype(F32)
        buffer[5, pl.ds(2, 1), pl.ds(0, 1)] = tally[...].astype(F32)
    pack_rows(tops, bottoms, x_ref, to_first, to_second, 0, 3)
    pack_rows(tops, bottoms, props, to_first, to_second, 3, 2)


def exchange_choice(levels, mates, choice):
    own = lax.axis_index("rep")
    mate = mates[own]
    near_mate = own + 1 - 2 * lax.rem(own, 2)
    row = (1, CA)
    ratio = jnp.full(row, levels[own], F32) / jnp.full(row, levels[mate], F32)
    choice[...] = jnp.zeros_like(choice)
    choice[pl.ds(0, 1), :] = jnp.full(row, jnp.where(mate == own, 1.0, 0.0), F32)
    choice[pl.ds(1, 1), :] = jnp.full(row, jnp.where(mate == near_mate, 1.0, 0.0), F32)
    choice[pl.ds(2, 1), :] = jnp.sqrt(ratio)


def local(
    atomic_locations,
    atomic_speeds,
    atomic_properties,
    resident_tile_members,
    resident_tile_tally,
    top_edge_groups,
    bottom_edge_groups,
    boundary_tile_slots,
    boundary_tile_tally,
    spring_links,
    thermal_levels,
    exchange_mate,
):
    atoms = atomic_locations.shape[2]
    clusters = atoms // CA
    facing = top_edge_groups.shape[1]
    shape = (3, clusters, CA)
    x = atomic_locations.reshape(shape)
    v = atomic_speeds.reshape(shape)
    pairs = resident_tile_members[:, 0]
    slots = boundary_tile_slots[:, 0]
    sds = jax.ShapeDtypeStruct
    params = pltpu.CompilerParams(vmem_limit_bytes=VMEM_LIMIT)

    to_first, to_second = pl.pallas_call(
        pack_kernel,
        out_shape=(sds((6, facing, CA), F32),) * 2,
        in_specs=[SMEM] * 2 + [VMEM] * 4,
        out_specs=(VMEM,) * 2,
        scratch_shapes=[pltpu.VMEM((2,) + shape[1:], F32)],
        compiler_params=pltpu.CompilerParams(vmem_limit_bytes=PACK_LIMIT),
        cost_estimate=pl.CostEstimate(
            flops=PACK_FLOPS * 1_000_000, bytes_accessed=1_000_000, transcendentals=0
        ),
        name="pack",
    )(
        top_edge_groups,
        bottom_edge_groups,
        x,
        atomic_properties,
        slots,
        boundary_tile_tally,
    )
    first_start = swapped(to_first, "dom", 0, True)
    second_start = swapped(to_second, "dom", 1, True)

    def scratch(sources):
        return [
            pltpu.VMEM((4, clusters * ROWS, CA), F32),
            pltpu.VMEM((clusters * ROWS, CA), F32),
            pltpu.VMEM((sources, 2 * ROWS, CA), BF16),
            pltpu.VMEM((sources, 2 * ROWS, CA), BF16),
        ]

    bonds = spring_links.shape[1]
    kept = (
        sds(shape, F32),
        sds((2, 2 * CA, bonds), BF16),
        sds((2, clusters // 2, bonds), BF16),
        sds((clusters, CA, CA), F32),
    )

    def local_call(first):
        sums = (
            sds((clusters * ROWS, CA), F32),
            sds(shape, F32),
            sds((clusters, 2, 2 * ROWS, CA), BF16),
            sds((clusters, CA), F32),
        )
        rows = 3 * clusters if first else 3 * clusters // 2
        return pl.pallas_call(
            functools.partial(local_kernel, first),
            out_shape=sums + kept if first else sums,
            in_specs=[SMEM] * 2 + [VMEM] * (3 if first else 7),
            out_specs=(VMEM,) * (8 if first else 4),
            scratch_shapes=scratch(clusters)
            + [
                pltpu.VMEM((rows, 2 * CA), BF16),
                pltpu.VMEM((rows, 2 * CA), F32),
            ],
            compiler_params=params,
            cost_estimate=pl.CostEstimate(
                flops=2_000_000_000, bytes_accessed=1_000_000, transcendentals=2_000_000
            ),
            name="resident",
        )

    def edge_call(first, last, kick):
        if last:
            outs = (sds((6, clusters, CA), F32), sds((ROWS, CA), F32))
        else:
            outs = (sds(shape, F32),) * 2 + (sds((3, facing, CA), F32),) * 2
        if first:
            outs += (sds((2 * facing, CA, CA), F32), sds((1, 1), jnp.int32))
        return pl.pallas_call(
            functools.partial(edge_kernel, first, last, kick),
            out_shape=outs,
            in_specs=[SMEM] * (6 if last else 5 if first else 4) + [VMEM] * (11 if first else 12),
            out_specs=(VMEM,) * (len(outs) - 1) + (SMEM if first else VMEM,),
            scratch_shapes=scratch(2 * facing)
            + [
                pltpu.VMEM((clusters * ROWS, CA), F32),
                pltpu.VMEM((ROWS, CA), jnp.int32),
                pltpu.SMEM((ROWS, CA), jnp.int32),
                pltpu.SemaphoreType.DMA,
            ],
            compiler_params=params,
            cost_estimate=pl.CostEstimate(
                flops=1_000_000_000, bytes_accessed=1_000_000, transcendentals=2_000_000
            ),
            name="edges",
        )

    halo_ratio = ()
    first_x, second_x = first_start, second_start
    for step in range(STEPS + 1):
        if step == 0:
            acc, bonded, far, rho, props, *static = local_call(True)(
                pairs, resident_tile_tally, x, atomic_properties, spring_links
            )
        else:
            acc, bonded, far, rho = local_call(False)(
                pairs, resident_tile_tally, x, props, x_before, bonded, *static
            )
        last = step == STEPS
        kick = TIME_STEP * (0.5 if step == 0 or last else 1.0)
        results = edge_call(step == 0, last, kick)(
            top_edge_groups,
            bottom_edge_groups,
            slots,
            boundary_tile_tally,
            *((thermal_levels, exchange_mate) if last else ()),
            *((exchange_mate,) if step == 0 else ()),
            x,
            v,
            props,
            acc,
            bonded,
            far,
            rho,
            first_x,
            second_x,
            first_start,
            second_start,
            *halo_ratio,
        )
        if last:
            state, choice = results
        else:
            x_before = x
            x, v, to_first, to_second, *new_ratio = results
            if step == 0:
                *halo_ratio, crossing = new_ratio
            first_x = swapped(to_first, "dom", 0, True)
            second_x = swapped(to_second, "dom", 1, True)

    keep, near_mate, ratio = choice[0] > 0.5, choice[1] > 0.5, choice[2]

    def chosen(own, one, two):
        return jnp.where(keep, own, jnp.where(near_mate, one, two))

    out = (3, 1, atoms)
    one = swapped(state, "rep", 0)
    two = lax.cond(
        crossing[0, 0] > 0, lambda s: swapped(s, "rep", 1), lambda s: jnp.zeros_like(s), state
    )
    new = chosen(state, one, two)
    return new[:3].reshape(out), (new[3:] * ratio).reshape(out)


def solution(mesh):
    placed = (
        P(None, "rep", "dom"),
        P(None, "rep", "dom"),
        P(None, "dom"),
        P(None, "rep", "dom"),
        P("rep", "dom"),
        P("rep", "dom"),
        P("rep", "dom"),
        P(None, "rep", "dom"),
        P("rep", "dom"),
        P(None, "dom"),
        P(),
        P(),
    )
    return jax.shard_map(
        local,
        mesh=mesh,
        in_specs=placed,
        out_specs=(P(None, "rep", "dom"), P(None, "rep", "dom")),
        check_vma=False,
    )
```

```python
import functools
import math

import jax
import jax.numpy as jnp
from jax import lax
from jax.experimental import pallas as pl
from jax.experimental.pallas import tpu as pltpu
from jax.sharding import PartitionSpec as P

CA = 128
STEPS = 2
TIME_STEP = 0.05

F32 = jnp.float32
BF16 = jnp.bfloat16
LOG2E = 1.4426950408889634
ROWS = 8
ROUNDS = 1
PIECES = 16
LAG_SCALE = 3
LAG_SUM = 6
EDGE_SCALE = 3
EDGE_SUM = 6
BOND_PULL = 2
BOND_SPREAD = 4
VMEM_LIMIT = 20 << 20
PACK_LIMIT = 60 << 20
PACK_FLOPS = 2000

SMEM = pl.BlockSpec(memory_space=pltpu.SMEM)
VMEM = pl.BlockSpec(memory_space=pltpu.VMEM)


def swapped(shard, axis, start, ring=False):
    devices = lax.axis_size(axis)
    pairs = []
    for i in range(start, devices if ring else devices - 1, 2):
        other = (i + 1) % devices
        pairs += [(i, other), (other, i)]
    return lax.ppermute(shard, axis, pairs)


def side_lists(tops, bottoms):
    odd = lax.rem(lax.axis_index("dom"), 2) == 1

    def first(k):
        return jnp.where(odd, bottoms[0, k], tops[0, k])

    def second(k):
        return jnp.where(odd, tops[0, k], bottoms[0, k])

    return odd, first, second


def halves(a):
    high = a.astype(BF16).astype(F32)
    return high, (a - high).astype(BF16).astype(F32)


def tile(cluster):
    return pl.ds(pl.multiple_of(cluster * ROWS, ROWS), ROWS)


def stack_rows(stack, base, rows):
    for k, row in enumerate(rows):
        count = rows[0].shape[0]
        if not hasattr(row, "shape"):
            row = jnp.full((count, CA), row, F32)
        stack[pl.ds(base * ROWS + k, count, stride=ROWS), :] = row


def position_parts(x, y, z):
    (xh, xm), (yh, ym), (zh, zm) = halves(x), halves(y), halves(z)
    x, y, z = xh + xm, yh + ym, zh + zm
    norm = x * x + y * y + z * z + 0.25
    nh, nm = halves(norm)
    return (xh, yh, zh), (xm, ym, zm), (nh, nm, norm - nh - nm)


def near_stack(stacks, base, high, middle, norm):
    stack_rows(stacks.at[0], base, [*high, norm[0], 1.0, 1.0, norm[2], 0.0])
    stack_rows(stacks.at[1], base, [*middle, norm[1], 0.0, 0.0, 0.0, 0.0])


def far_stack(stacks, high, middle, norm):
    twice = [-2.0 * a for a in high]
    stack_rows(stacks.at[2], 0, [*twice, 1.0, norm[0], norm[2], 1.0, 0.0])
    stack_rows(stacks.at[3], 0, [*[-2.0 * a for a in middle], 0.0, norm[1], 0.0, 0.0, 0.0])


def fill_ratio(ratio, rho, base):
    for c in range(rho.shape[0]):
        ratio[base + c] = jnp.transpose(jnp.broadcast_to(rho[c : c + 1], (CA, CA)))


def moment_stack(stack, base, x, y, z, strength):
    g = strength * math.exp(0.25)
    parts = [halves(a) for a in (g * x, g * y, g * z, g)]
    stack_rows(stack, base, [p[0] for p in parts] + [p[1] for p in parts])


def both_orders(stacks, k, c):
    h, m = stacks[k, tile(c), :], stacks[k + 1, tile(c), :]
    return (
        jnp.concatenate([h, m], axis=0).astype(BF16),
        jnp.concatenate([m, h], axis=0).astype(BF16),
    )


def fill_near(near, stacks, c):
    near[c] = both_orders(stacks, 0, c)[0]


def fill_far(far, stacks, c):
    far[c, 0], far[c, 1] = both_orders(stacks, 2, c)


def fill_moments(moments, stack, c):
    w = stack[tile(c), :]
    moments[c] = jnp.concatenate([w, jnp.zeros_like(w)], axis=0).astype(BF16)


def distances(near, far, pair, other):
    left = [near[i] for i, _ in (pair, other)]
    left = jnp.transpose(jnp.concatenate([left[0], left[0], left[1], left[1]], axis=0))
    right = [jnp.concatenate([far[j, 0], far[j, 1]], axis=0) for _, j in (pair, other)]
    zero = jnp.zeros_like(right[0])
    right = jnp.concatenate(
        [
            jnp.concatenate([right[0], zero], axis=1),
            jnp.concatenate([zero, right[1]], axis=1),
        ],
        axis=0,
    )
    both = jnp.dot(left, right, preferred_element_type=F32)
    return both[:, :CA], both[:, CA:]


def charge_ratio(charge, strength):
    return charge / strength * math.exp(-0.125)


def pair_scale(t, near_rho, far_rho):
    r = lax.rsqrt(t)
    c = jnp.exp2(t * (-0.5 * LOG2E)) + (near_rho * far_rho) * (r * r * r)
    high = c.astype(BF16)
    return high, (c - high.astype(F32)).astype(BF16)


def moment_sums(weights, scales):
    sums = jnp.dot(weights, scales, preferred_element_type=F32)[:ROWS]
    return sums[:, :CA] + sums[:, CA:]


def split(a, parts):
    return halves(a) if parts == 2 else (a,)


def bond_table(x, parts):
    half = x.shape[1] // 2

    def lay(v):
        flat = (3 * half, CA)
        return jnp.concatenate([v[:, :half].reshape(flat), v[:, half:].reshape(flat)], axis=1)

    return jnp.concatenate([lay(part) for part in split(x, parts)], axis=0).astype(BF16)


def bond_picks(picks, masks, atoms, start):
    size = atoms.shape[1]
    half = masks.shape[1]
    lane_id = lax.broadcasted_iota(jnp.int32, (2 * CA, size), 0).astype(F32).astype(BF16)
    row_id = lax.broadcasted_iota(jnp.int32, (half, size), 0)
    one, none = jnp.ones((), BF16), jnp.zeros((), BF16)
    for e in range(2):
        atom = atoms[e : e + 1]
        cluster = atom // CA
        lane = (atom % CA + cluster // half * CA).astype(F32).astype(BF16)
        hit = lane_id == jnp.broadcast_to(lane, lane_id.shape)
        picks[e, :, pl.ds(start, size)] = jnp.where(hit, one, none)
        mask = jnp.where(row_id == cluster % half, 1.0, 0.0)
        masks[e, :, pl.ds(start, size)] = mask.astype(BF16)


def bond_gather(table, picks, start, size):
    return [
        jnp.dot(table, picks[e, :, pl.ds(start, size)], preferred_element_type=F32)
        for e in range(2)
    ]


def bond_pull(rows, masks, start, size):
    half = masks.shape[1]
    parts = rows[0].shape[0] // (3 * half)
    ends = []
    for e in range(2):
        mask = masks[e, :, pl.ds(start, size)].astype(F32)
        both = sum(rows[e][k * 3 * half : (k + 1) * 3 * half] for k in range(parts))
        ends.append(jnp.sum(both.reshape(3, half, size) * mask[None], axis=1))
    return split(ends[1] - ends[0], parts)


def bond_scatter(pull, picks, masks, start, size):
    half = masks.shape[1]
    total = None
    for e, sign in enumerate((1.0, -1.0)):
        mask = masks[e, :, pl.ds(start, size)]
        spread = [
            mask * jnp.broadcast_to(sign * part[c : c + 1], (half, size)).astype(BF16)
            for part in pull
            for c in range(3)
        ]
        term = lax.dot_general(
            jnp.concatenate(spread, axis=0),
            picks[e, :, pl.ds(start, size)],
            (((1,), (1,)), ((), ())),
            preferred_element_type=F32,
        )
        total = term if total is None else total + term
    return total


def pair_moments(moments, i, j, scale):
    high, low = scale
    on_far = moment_sums(moments[i], jnp.concatenate([high, low], axis=1))
    turned = jnp.concatenate([jnp.transpose(high), jnp.transpose(low)], axis=1)
    return moment_sums(moments[j], turned), on_far


def local_kernel(first, pairs, tally, x_ref, props, *rest):
    if first:
        raw = props
        bonds, acc, bonded, far, rho, props, picks, masks, ratio, *scratch = rest
        relay_properties(raw, props)
    else:
        x_before, bonded_before, picks, masks, ratio, acc, bonded, far, rho, *scratch = rest
    stacks, moment_rows, near, moments, table, bond_sums = scratch
    clusters = x_ref.shape[1]
    half = clusters // 2
    group = pairs.shape[1] // ROUNDS
    size = picks.shape[2] // ROUNDS
    x, y, z = x_ref[0], x_ref[1], x_ref[2]
    parts = position_parts(x, y, z)
    rho[...] = charge_ratio(props[0], props[1])
    if first:
        fill_ratio(ratio, rho[...], 0)
    near_stack(stacks, 0, *parts)
    far_stack(stacks, *parts)
    moment_stack(moment_rows, 0, x, y, z, props[1])
    for c in range(clusters):
        fill_near(near, stacks, c)
        fill_far(far, stacks, c)
        fill_moments(moments, moment_rows, c)
    acc[...] = jnp.zeros_like(acc)
    if first:
        table[...] = bond_table(x_ref[...], 2)
    else:
        table[...] = bond_table(x_ref[...] - x_before[...], 1)
    bond_sums[...] = jnp.zeros_like(bond_sums)
    live = jnp.broadcast_to(tally[...], (ROWS, CA))

    def round_of(block, carry):
        start = pl.multiple_of(block * size, size)
        if first:
            bond_picks(picks, masks, bonds[:, pl.ds(start, size)], start)
        slots = [block * group + k for k in range(group)]
        ends = [(pairs[0, s], pairs[1, s]) for s in slots]
        piece = size // PIECES
        steps = group // PIECES
        products, scales, sums = [None] * group, [None] * group, [None] * group
        gathered, pulls, spread = [None] * PIECES, [None] * PIECES, None
        for t in range(group + LAG_SUM):
            if t < group and t % 2 == 0:
                products[t : t + 2] = distances(near, far, ends[t], ends[t + 1])
            q = t // steps
            if t % steps == 0 and q < PIECES:
                gathered[q] = bond_gather(table[...], picks, start + q * piece, piece)
            q = (t - BOND_PULL) // steps
            if (t - BOND_PULL) % steps == 0 and 0 <= q < PIECES:
                pulls[q] = bond_pull(gathered[q], masks, start + q * piece, piece)
            q = t - LAG_SCALE
            if 0 <= q < group:
                i, j = ends[q]
                scales[q] = pair_scale(products[q], ratio[i], rho[pl.ds(j, 1), :])
            q = t - LAG_SUM
            if 0 <= q < group:
                sums[q] = pair_moments(moments, *ends[q], scales[q])
            q = (t - BOND_SPREAD) // steps
            if (t - BOND_SPREAD) % steps == 0 and 0 <= q < PIECES:
                part = bond_scatter(pulls[q], picks, masks, start + q * piece, piece)
                spread = part if spread is None else spread + part
        bond_sums[...] += spread
        for s, (i, j), (on_near, on_far) in zip(slots, ends, sums):
            weight = jnp.where(live > s, jnp.where(i == j, 0.5, 1.0), 0.0)
            acc[tile(i), :] += weight * on_near
            acc[tile(j), :] += weight * on_far
        return carry

    lax.fori_loop(0, ROUNDS, round_of, 0)
    for c in range(3):
        both = bond_sums[pl.ds(c * half, half), :]
        if first:
            both = both + bond_sums[pl.ds((3 + c) * half, half), :]
        for k in range(2):
            new = both[:, k * CA : (k + 1) * CA]
            if not first:
                new = new + bonded_before[c, pl.ds(k * half, half), :]
            bonded[c, pl.ds(k * half, half), :] = new


def edge_kernel(first, last, kick, tops, bottoms, slots, *rest):
    if last:
        levels, mates, *rest = rest
    tally, x_ref, v_ref, props, acc_in, bonded, far, rho, *rest = rest
    first_x, second_x, first_start, second_start, *rest = rest
    *rest, stacks, moment_rows, near, moments, acc, indices, lower, arrived = rest
    if last:
        ratio, state, choice = rest
        exchange_choice(levels, mates, choice)
    elif first:
        x_out, v_out, to_first, to_second, ratio = rest
    else:
        ratio, x_out, v_out, to_first, to_second = rest
    odd, _, _ = side_lists(tops, bottoms)
    rows = [start[5, pl.ds(0, ROWS), :] for start in (first_start, second_start)]
    indices[...] = jnp.where(odd, rows[0], rows[1]).astype(jnp.int32)
    indices[pl.ds(3, 1), pl.ds(0, 1)] = tally[...]
    fetch = pltpu.make_async_copy(indices, lower, arrived)
    fetch.start()
    clusters = x_ref.shape[1]
    facing = first_x.shape[1]
    for side, (hx, hp) in enumerate(((first_x, first_start), (second_x, second_start))):
        if first:
            fill_ratio(ratio, charge_ratio(hp[3], hp[4]), side * facing)
        near_stack(stacks, side * facing, *position_parts(hx[0], hx[1], hx[2]))
        moment_stack(moment_rows, side * facing, hx[0], hx[1], hx[2], hp[4])
    for c in range(2 * facing):
        fill_near(near, stacks, c)
        fill_moments(moments, moment_rows, c)
    acc[...] = acc_in[...]

    width = slots.shape[1]
    upper_base = jnp.where(odd, facing, 0)
    lower_base = facing - upper_base
    fetch.wait()
    ends, weights = [], []
    for s in range(width):
        ends.append((upper_base + slots[1, s], tops[0, slots[0, s]]))
        weights.append(jnp.where(s < lower[3, 0], 1.0, 0.0))
        ends.append((lower_base + lower[0, s], bottoms[0, lower[1, s]]))
        weights.append(jnp.where(s < lower[2, 0], 1.0, 0.0))
    count = len(ends)
    products, scales = [None] * count, [None] * count
    for t in range(count + EDGE_SUM):
        if t < count and t % 2 == 0:
            products[t : t + 2] = distances(near, far, ends[t], ends[t + 1])
        q = t - EDGE_SCALE
        if 0 <= q < count:
            j, i = ends[q]
            scales[q] = pair_scale(products[q], ratio[j], rho[pl.ds(i, 1), :])
        q = t - EDGE_SUM
        if 0 <= q < count:
            j, i = ends[q]
            total = moment_sums(moments[j], jnp.concatenate(scales[q], axis=1))
            acc[tile(i), :] += weights[q] * total

    def moment(k):
        high = acc[pl.ds(k, clusters, stride=ROWS), :]
        return high + acc[pl.ds(k + 4, clusters, stride=ROWS), :]

    mass = kick * props[2]
    g = props[1]
    count = moment(3)
    for c in range(3):
        force = g * (x_ref[c] * count - moment(c)) + bonded[c]
        v = v_ref[c] + mass * force
        if last:
            state[c] = x_ref[c]
            state[3 + c] = v
        else:
            v_out[c] = v
            x_out[c] = x_ref[c] + TIME_STEP * v
    if not last:
        pack_rows(tops, bottoms, x_out, to_first, to_second, 0, 3)


def pack_rows(tops, bottoms, source, to_first, to_second, base, count):
    _, first, second = side_lists(tops, bottoms)
    for k in range(to_first.shape[1]):
        i, j = first(k), second(k)
        rows = [[source[c, pl.ds(n, 1), :] for c in range(count)] for n in (i, j)]
        for c in range(count):
            to_first[base + c, pl.ds(k, 1), :] = rows[0][c]
            to_second[base + c, pl.ds(k, 1), :] = rows[1][c]


def relay_properties(raw, props):
    for c in range(props.shape[0]):
        for k in range(props.shape[1]):
            props[c, pl.ds(k, 1), :] = raw[pl.ds(c, 1), pl.ds(k * CA, CA)]


def pack_kernel(tops, bottoms, x_ref, raw, slots, tally, to_first, to_second, props):
    relay_properties(raw, props)
    width = slots.shape[1]
    for buffer in (to_first, to_second):
        buffer[5] = jnp.zeros(buffer.shape[1:], F32)
        buffer[5, pl.ds(0, 2), pl.ds(0, width)] = slots[...].astype(F32)
        buffer[5, pl.ds(2, 1), pl.ds(0, 1)] = tally[...].astype(F32)
    pack_rows(tops, bottoms, x_ref, to_first, to_second, 0, 3)
    pack_rows(tops, bottoms, props, to_first, to_second, 3, 2)


def exchange_choice(levels, mates, choice):
    own = lax.axis_index("rep")
    mate = mates[own]
    near_mate = own + 1 - 2 * lax.rem(own, 2)
    row = (1, CA)
    ratio = jnp.full(row, levels[own], F32) / jnp.full(row, levels[mate], F32)
    choice[...] = jnp.zeros_like(choice)
    choice[pl.ds(0, 1), :] = jnp.full(row, jnp.where(mate == own, 1.0, 0.0), F32)
    choice[pl.ds(1, 1), :] = jnp.full(row, jnp.where(mate == near_mate, 1.0, 0.0), F32)
    choice[pl.ds(2, 1), :] = jnp.sqrt(ratio)


def local(
    atomic_locations,
    atomic_speeds,
    atomic_properties,
    resident_tile_members,
    resident_tile_tally,
    top_edge_groups,
    bottom_edge_groups,
    boundary_tile_slots,
    boundary_tile_tally,
    spring_links,
    thermal_levels,
    exchange_mate,
):
    atoms = atomic_locations.shape[2]
    clusters = atoms // CA
    facing = top_edge_groups.shape[1]
    shape = (3, clusters, CA)
    x = atomic_locations.reshape(shape)
    v = atomic_speeds.reshape(shape)
    pairs = resident_tile_members[:, 0]
    slots = boundary_tile_slots[:, 0]
    sds = jax.ShapeDtypeStruct
    params = pltpu.CompilerParams(vmem_limit_bytes=VMEM_LIMIT)

    to_first, to_second = pl.pallas_call(
        pack_kernel,
        out_shape=(sds((6, facing, CA), F32),) * 2,
        in_specs=[SMEM] * 2 + [VMEM] * 4,
        out_specs=(VMEM,) * 2,
        scratch_shapes=[pltpu.VMEM((2,) + shape[1:], F32)],
        compiler_params=pltpu.CompilerParams(vmem_limit_bytes=PACK_LIMIT),
        cost_estimate=pl.CostEstimate(
            flops=PACK_FLOPS * 1_000_000, bytes_accessed=1_000_000, transcendentals=0
        ),
        name="pack",
    )(
        top_edge_groups,
        bottom_edge_groups,
        x,
        atomic_properties,
        slots,
        boundary_tile_tally,
    )
    first_start = swapped(to_first, "dom", 0, True)
    second_start = swapped(to_second, "dom", 1, True)

    def scratch(sources):
        return [
            pltpu.VMEM((4, clusters * ROWS, CA), F32),
            pltpu.VMEM((clusters * ROWS, CA), F32),
            pltpu.VMEM((sources, 2 * ROWS, CA), BF16),
            pltpu.VMEM((sources, 2 * ROWS, CA), BF16),
        ]

    bonds = spring_links.shape[1]
    kept = (
        sds(shape, F32),
        sds((2, 2 * CA, bonds), BF16),
        sds((2, clusters // 2, bonds), BF16),
        sds((clusters, CA, CA), F32),
    )

    def local_call(first):
        sums = (
            sds((clusters * ROWS, CA), F32),
            sds(shape, F32),
            sds((clusters, 2, 2 * ROWS, CA), BF16),
            sds((clusters, CA), F32),
        )
        rows = 3 * clusters if first else 3 * clusters // 2
        return pl.pallas_call(
            functools.partial(local_kernel, first),
            out_shape=sums + kept if first else sums,
            in_specs=[SMEM] + [VMEM] * (4 if first else 8),
            out_specs=(VMEM,) * (8 if first else 4),
            scratch_shapes=scratch(clusters)
            + [
                pltpu.VMEM((rows, 2 * CA), BF16),
                pltpu.VMEM((rows, 2 * CA), F32),
            ],
            compiler_params=params,
            cost_estimate=pl.CostEstimate(
                flops=2_000_000_000, bytes_accessed=1_000_000, transcendentals=2_000_000
            ),
            name="resident",
        )

    def edge_call(first, last, kick):
        if last:
            outs = (sds((6, clusters, CA), F32), sds((ROWS, CA), F32))
        else:
            outs = (sds(shape, F32),) * 2 + (sds((3, facing, CA), F32),) * 2
        if first:
            outs += (sds((2 * facing, CA, CA), F32),)
        return pl.pallas_call(
            functools.partial(edge_kernel, first, last, kick),
            out_shape=outs,
            in_specs=[SMEM] * (5 if last else 3) + [VMEM] * (12 if first else 13),
            out_specs=(VMEM,) * len(outs),
            scratch_shapes=scratch(2 * facing)
            + [
                pltpu.VMEM((clusters * ROWS, CA), F32),
                pltpu.VMEM((ROWS, CA), jnp.int32),
                pltpu.SMEM((ROWS, CA), jnp.int32),
                pltpu.SemaphoreType.DMA,
            ],
            compiler_params=params,
            cost_estimate=pl.CostEstimate(
                flops=1_000_000_000, bytes_accessed=1_000_000, transcendentals=2_000_000
            ),
            name="edges",
        )

    halo_ratio = ()
    first_x, second_x = first_start, second_start
    for step in range(STEPS + 1):
        if step == 0:
            acc, bonded, far, rho, props, *static = local_call(True)(
                pairs, resident_tile_tally, x, atomic_properties, spring_links
            )
        else:
            acc, bonded, far, rho = local_call(False)(
                pairs, resident_tile_tally, x, props, x_before, bonded, *static
            )
        last = step == STEPS
        kick = TIME_STEP * (0.5 if step == 0 or last else 1.0)
        results = edge_call(step == 0, last, kick)(
            top_edge_groups,
            bottom_edge_groups,
            slots,
            *((thermal_levels, exchange_mate) if last else ()),
            boundary_tile_tally,
            x,
            v,
            props,
            acc,
            bonded,
            far,
            rho,
            first_x,
            second_x,
            first_start,
            second_start,
            *halo_ratio,
        )
        if last:
            state, choice = results
        else:
            x_before = x
            x, v, to_first, to_second, *new_ratio = results
            halo_ratio = halo_ratio or new_ratio
            first_x = swapped(to_first, "dom", 0, True)
            second_x = swapped(to_second, "dom", 1, True)

    keep, near_mate, ratio = choice[0] > 0.5, choice[1] > 0.5, choice[2]
    slot = jnp.arange(exchange_mate.shape[0], dtype=jnp.int32)
    crossing = jnp.any((exchange_mate != slot) & (exchange_mate != (slot ^ 1)))

    def exchanged(state, *others):
        def part(k):
            own, *rest = [a[3 * k : 3 * k + 3] for a in (state, *others)]
            other = jnp.where(near_mate, *rest) if len(rest) == 2 else rest[0]
            return jnp.where(keep, own, other)

        return part(0), part(1) * ratio

    def with_crossing(state):
        return exchanged(state, swapped(state, "rep", 0), swapped(state, "rep", 1))

    def without_crossing(state):
        return exchanged(state, swapped(state, "rep", 0))

    new_x, new_v = lax.cond(crossing, with_crossing, without_crossing, state)
    return new_x.reshape(3, 1, atoms), new_v.reshape(3, 1, atoms)


def solution(mesh):
    placed = (
        P(None, "rep", "dom"),
        P(None, "rep", "dom"),
        P(None, "dom"),
        P(None, "rep", "dom"),
        P("rep", "dom"),
        P("rep", "dom"),
        P("rep", "dom"),
        P(None, "rep", "dom"),
        P("rep", "dom"),
        P(None, "dom"),
        P(),
        P(),
    )
    return jax.shard_map(
        local,
        mesh=mesh,
        in_specs=placed,
        out_specs=(P(None, "rep", "dom"), P(None, "rep", "dom")),
        check_vma=False,
    )
```

```python
import functools
import math

import jax
import jax.numpy as jnp
from jax import lax
from jax.experimental import pallas as pl
from jax.experimental.pallas import tpu as pltpu
from jax.sharding import PartitionSpec as P

CA = 128
STEPS = 2
TIME_STEP = 0.05

F32 = jnp.float32
BF16 = jnp.bfloat16
LOG2E = 1.4426950408889634
ROWS = 8
ROUNDS = 1
PIECES = 16
LAG_SCALE = 3
LAG_SUM = 6
EDGE_SCALE = 3
EDGE_SUM = 6
BOND_PULL = 2
BOND_SPREAD = 4
VMEM_LIMIT = 20 << 20
PACK_LIMIT = 60 << 20
PACK_FLOPS = 2000

SMEM = pl.BlockSpec(memory_space=pltpu.SMEM)
VMEM = pl.BlockSpec(memory_space=pltpu.VMEM)


def swapped(shard, axis, start, ring=False):
    devices = lax.axis_size(axis)
    pairs = []
    for i in range(start, devices if ring else devices - 1, 2):
        other = (i + 1) % devices
        pairs += [(i, other), (other, i)]
    return lax.ppermute(shard, axis, pairs)


def side_lists(tops, bottoms):
    odd = lax.rem(lax.axis_index("dom"), 2) == 1

    def first(k):
        return jnp.where(odd, bottoms[0, k], tops[0, k])

    def second(k):
        return jnp.where(odd, tops[0, k], bottoms[0, k])

    return odd, first, second


def halves(a):
    high = a.astype(BF16).astype(F32)
    return high, (a - high).astype(BF16).astype(F32)


def tile(cluster):
    return pl.ds(pl.multiple_of(cluster * ROWS, ROWS), ROWS)


def stack_rows(stack, base, rows):
    for k, row in enumerate(rows):
        count = rows[0].shape[0]
        if not hasattr(row, "shape"):
            row = jnp.full((count, CA), row, F32)
        stack[pl.ds(base * ROWS + k, count, stride=ROWS), :] = row


def position_parts(x, y, z):
    (xh, xm), (yh, ym), (zh, zm) = halves(x), halves(y), halves(z)
    x, y, z = xh + xm, yh + ym, zh + zm
    norm = x * x + y * y + z * z + 0.25
    nh, nm = halves(norm)
    return (xh, yh, zh), (xm, ym, zm), (nh, nm, norm - nh - nm)


def near_stack(stacks, base, high, middle, norm):
    stack_rows(stacks.at[0], base, [*high, norm[0], 1.0, 1.0, norm[2], 0.0])
    stack_rows(stacks.at[1], base, [*middle, norm[1], 0.0, 0.0, 0.0, 0.0])


def far_stack(stacks, high, middle, norm):
    twice = [-2.0 * a for a in high]
    stack_rows(stacks.at[2], 0, [*twice, 1.0, norm[0], norm[2], 1.0, 0.0])
    stack_rows(stacks.at[3], 0, [*[-2.0 * a for a in middle], 0.0, norm[1], 0.0, 0.0, 0.0])


def fill_ratio(ratio, rho, base):
    for c in range(rho.shape[0]):
        ratio[base + c] = jnp.transpose(jnp.broadcast_to(rho[c : c + 1], (CA, CA)))


def moment_stack(stack, base, x, y, z, strength):
    g = strength * math.exp(0.25)
    parts = [halves(a) for a in (g * x, g * y, g * z, g)]
    stack_rows(stack, base, [p[0] for p in parts] + [p[1] for p in parts])


def both_orders(stacks, k, c):
    h, m = stacks[k, tile(c), :], stacks[k + 1, tile(c), :]
    return (
        jnp.concatenate([h, m], axis=0).astype(BF16),
        jnp.concatenate([m, h], axis=0).astype(BF16),
    )


def fill_near(near, stacks, c):
    near[c] = both_orders(stacks, 0, c)[0]


def fill_far(far, stacks, c):
    far[c, 0], far[c, 1] = both_orders(stacks, 2, c)


def fill_moments(moments, stack, c):
    w = stack[tile(c), :]
    moments[c] = jnp.concatenate([w, jnp.zeros_like(w)], axis=0).astype(BF16)


def distances(near, far, pair, other):
    left = [near[i] for i, _ in (pair, other)]
    left = jnp.transpose(jnp.concatenate([left[0], left[0], left[1], left[1]], axis=0))
    right = [jnp.concatenate([far[j, 0], far[j, 1]], axis=0) for _, j in (pair, other)]
    zero = jnp.zeros_like(right[0])
    right = jnp.concatenate(
        [
            jnp.concatenate([right[0], zero], axis=1),
            jnp.concatenate([zero, right[1]], axis=1),
        ],
        axis=0,
    )
    both = jnp.dot(left, right, preferred_element_type=F32)
    return both[:, :CA], both[:, CA:]


def charge_ratio(charge, strength):
    return charge / strength * math.exp(-0.125)


def pair_scale(t, near_rho, far_rho):
    r = lax.rsqrt(t)
    c = jnp.exp2(t * (-0.5 * LOG2E)) + (near_rho * far_rho) * (r * r * r)
    high = c.astype(BF16)
    return high, (c - high.astype(F32)).astype(BF16)


def moment_sums(weights, scales):
    sums = jnp.dot(weights, scales, preferred_element_type=F32)[:ROWS]
    return sums[:, :CA] + sums[:, CA:]


def split(a, parts):
    return halves(a) if parts == 2 else (a,)


def bond_table(x, parts):
    half = x.shape[1] // 2

    def lay(v):
        flat = (3 * half, CA)
        return jnp.concatenate([v[:, :half].reshape(flat), v[:, half:].reshape(flat)], axis=1)

    return jnp.concatenate([lay(part) for part in split(x, parts)], axis=0).astype(BF16)


def bond_picks(picks, masks, atoms, start):
    size = atoms.shape[1]
    half = masks.shape[1]
    lane_id = lax.broadcasted_iota(jnp.int32, (2 * CA, size), 0).astype(F32).astype(BF16)
    row_id = lax.broadcasted_iota(jnp.int32, (half, size), 0)
    one, none = jnp.ones((), BF16), jnp.zeros((), BF16)
    for e in range(2):
        atom = atoms[e : e + 1]
        cluster = atom // CA
        lane = (atom % CA + cluster // half * CA).astype(F32).astype(BF16)
        hit = lane_id == jnp.broadcast_to(lane, lane_id.shape)
        picks[e, :, pl.ds(start, size)] = jnp.where(hit, one, none)
        mask = jnp.where(row_id == cluster % half, 1.0, 0.0)
        masks[e, :, pl.ds(start, size)] = mask.astype(BF16)


def bond_gather(table, picks, start, size):
    return [
        jnp.dot(table, picks[e, :, pl.ds(start, size)], preferred_element_type=F32)
        for e in range(2)
    ]


def bond_pull(rows, masks, start, size):
    half = masks.shape[1]
    parts = rows[0].shape[0] // (3 * half)
    ends = []
    for e in range(2):
        mask = masks[e, :, pl.ds(start, size)].astype(F32)
        both = sum(rows[e][k * 3 * half : (k + 1) * 3 * half] for k in range(parts))
        ends.append(jnp.sum(both.reshape(3, half, size) * mask[None], axis=1))
    return split(ends[1] - ends[0], parts)


def bond_scatter(pull, picks, masks, start, size):
    half = masks.shape[1]
    total = None
    for e, sign in enumerate((1.0, -1.0)):
        mask = masks[e, :, pl.ds(start, size)]
        spread = [
            mask * jnp.broadcast_to(sign * part[c : c + 1], (half, size)).astype(BF16)
            for part in pull
            for c in range(3)
        ]
        term = lax.dot_general(
            jnp.concatenate(spread, axis=0),
            picks[e, :, pl.ds(start, size)],
            (((1,), (1,)), ((), ())),
            preferred_element_type=F32,
        )
        total = term if total is None else total + term
    return total


def pair_moments(moments, i, j, scale):
    high, low = scale
    on_far = moment_sums(moments[i], jnp.concatenate([high, low], axis=1))
    turned = jnp.concatenate([jnp.transpose(high), jnp.transpose(low)], axis=1)
    return moment_sums(moments[j], turned), on_far


def local_kernel(first, pairs, tally, x_ref, props, *rest):
    if first:
        raw = props
        bonds, acc, bonded, far, rho, props, picks, masks, ratio, *scratch = rest
        relay_properties(raw, props)
    else:
        x_before, bonded_before, picks, masks, ratio, acc, bonded, far, rho, *scratch = rest
    stacks, moment_rows, near, moments, table, bond_sums = scratch
    clusters = x_ref.shape[1]
    half = clusters // 2
    group = pairs.shape[1] // ROUNDS
    size = picks.shape[2] // ROUNDS
    x, y, z = x_ref[0], x_ref[1], x_ref[2]
    parts = position_parts(x, y, z)
    rho[...] = charge_ratio(props[0], props[1])
    if first:
        fill_ratio(ratio, rho[...], 0)
    near_stack(stacks, 0, *parts)
    far_stack(stacks, *parts)
    moment_stack(moment_rows, 0, x, y, z, props[1])
    for c in range(clusters):
        fill_near(near, stacks, c)
        fill_far(far, stacks, c)
        fill_moments(moments, moment_rows, c)
    acc[...] = jnp.zeros_like(acc)
    if first:
        table[...] = bond_table(x_ref[...], 2)
    else:
        table[...] = bond_table(x_ref[...] - x_before[...], 1)
    bond_sums[...] = jnp.zeros_like(bond_sums)
    live = jnp.broadcast_to(tally[...], (ROWS, CA))

    def round_of(block, carry):
        start = pl.multiple_of(block * size, size)
        if first:
            bond_picks(picks, masks, bonds[:, pl.ds(start, size)], start)
        slots = [block * group + k for k in range(group)]
        ends = [(pairs[0, s], pairs[1, s]) for s in slots]
        piece = size // PIECES
        steps = group // PIECES
        products, scales, sums = [None] * group, [None] * group, [None] * group
        gathered, pulls, spread = [None] * PIECES, [None] * PIECES, None
        for t in range(group + LAG_SUM):
            if t < group and t % 2 == 0:
                products[t : t + 2] = distances(near, far, ends[t], ends[t + 1])
            q = t // steps
            if t % steps == 0 and q < PIECES:
                gathered[q] = bond_gather(table[...], picks, start + q * piece, piece)
            q = (t - BOND_PULL) // steps
            if (t - BOND_PULL) % steps == 0 and 0 <= q < PIECES:
                pulls[q] = bond_pull(gathered[q], masks, start + q * piece, piece)
            q = t - LAG_SCALE
            if 0 <= q < group:
                i, j = ends[q]
                scales[q] = pair_scale(products[q], ratio[i], rho[pl.ds(j, 1), :])
            q = t - LAG_SUM
            if 0 <= q < group:
                sums[q] = pair_moments(moments, *ends[q], scales[q])
            q = (t - BOND_SPREAD) // steps
            if (t - BOND_SPREAD) % steps == 0 and 0 <= q < PIECES:
                part = bond_scatter(pulls[q], picks, masks, start + q * piece, piece)
                spread = part if spread is None else spread + part
        bond_sums[...] += spread
        for s, (i, j), (on_near, on_far) in zip(slots, ends, sums):
            weight = jnp.where(live > s, jnp.where(i == j, 0.5, 1.0), 0.0)
            acc[tile(i), :] += weight * on_near
            acc[tile(j), :] += weight * on_far
        return carry

    lax.fori_loop(0, ROUNDS, round_of, 0)
    for c in range(3):
        both = bond_sums[pl.ds(c * half, half), :]
        if first:
            both = both + bond_sums[pl.ds((3 + c) * half, half), :]
        for k in range(2):
            new = both[:, k * CA : (k + 1) * CA]
            if not first:
                new = new + bonded_before[c, pl.ds(k * half, half), :]
            bonded[c, pl.ds(k * half, half), :] = new


def edge_kernel(first, last, kick, tops, bottoms, slots, *rest):
    if last:
        levels, mates, *rest = rest
    tally, x_ref, v_ref, props, acc_in, bonded, far, rho, *rest = rest
    first_x, second_x, first_start, second_start, *rest = rest
    *rest, stacks, moment_rows, near, moments, acc, indices, lower, arrived = rest
    if last:
        ratio, state, choice = rest
        exchange_choice(levels, mates, choice)
    elif first:
        x_out, v_out, to_first, to_second, ratio = rest
    else:
        ratio, x_out, v_out, to_first, to_second = rest
    odd, _, _ = side_lists(tops, bottoms)
    rows = [start[5, pl.ds(0, ROWS), :] for start in (first_start, second_start)]
    indices[...] = jnp.where(odd, rows[0], rows[1]).astype(jnp.int32)
    indices[pl.ds(3, 1), pl.ds(0, 1)] = tally[...]
    fetch = pltpu.make_async_copy(indices, lower, arrived)
    fetch.start()
    clusters = x_ref.shape[1]
    facing = first_x.shape[1]
    for side, (hx, hp) in enumerate(((first_x, first_start), (second_x, second_start))):
        if first:
            fill_ratio(ratio, charge_ratio(hp[3], hp[4]), side * facing)
        near_stack(stacks, side * facing, *position_parts(hx[0], hx[1], hx[2]))
        moment_stack(moment_rows, side * facing, hx[0], hx[1], hx[2], hp[4])
    for c in range(2 * facing):
        fill_near(near, stacks, c)
        fill_moments(moments, moment_rows, c)
    acc[...] = acc_in[...]

    width = slots.shape[1]
    upper_base = jnp.where(odd, facing, 0)
    lower_base = facing - upper_base
    fetch.wait()
    ends, weights = [], []
    for s in range(width):
        ends.append((upper_base + slots[1, s], tops[0, slots[0, s]]))
        weights.append(jnp.where(s < lower[3, 0], 1.0, 0.0))
        ends.append((lower_base + lower[0, s], bottoms[0, lower[1, s]]))
        weights.append(jnp.where(s < lower[2, 0], 1.0, 0.0))
    count = len(ends)
    products, scales = [None] * count, [None] * count
    for t in range(count + EDGE_SUM):
        if t < count and t % 2 == 0:
            products[t : t + 2] = distances(near, far, ends[t], ends[t + 1])
        q = t - EDGE_SCALE
        if 0 <= q < count:
            j, i = ends[q]
            scales[q] = pair_scale(products[q], ratio[j], rho[pl.ds(i, 1), :])
        q = t - EDGE_SUM
        if 0 <= q < count:
            j, i = ends[q]
            total = moment_sums(moments[j], jnp.concatenate(scales[q], axis=1))
            acc[tile(i), :] += weights[q] * total

    def moment(k):
        high = acc[pl.ds(k, clusters, stride=ROWS), :]
        return high + acc[pl.ds(k + 4, clusters, stride=ROWS), :]

    mass = kick * props[2]
    g = props[1]
    count = moment(3)
    for c in range(3):
        force = g * (x_ref[c] * count - moment(c)) + bonded[c]
        v = v_ref[c] + mass * force
        if last:
            state[c] = x_ref[c]
            state[3 + c] = v
        else:
            v_out[c] = v
            x_out[c] = x_ref[c] + TIME_STEP * v
    if not last:
        pack_rows(tops, bottoms, x_out, to_first, to_second, 0, 3)


def pack_rows(tops, bottoms, source, to_first, to_second, base, count):
    _, first, second = side_lists(tops, bottoms)
    for k in range(to_first.shape[1]):
        i, j = first(k), second(k)
        rows = [[source[c, pl.ds(n, 1), :] for c in range(count)] for n in (i, j)]
        for c in range(count):
            to_first[base + c, pl.ds(k, 1), :] = rows[0][c]
            to_second[base + c, pl.ds(k, 1), :] = rows[1][c]


def relay_properties(raw, props):
    for c in range(props.shape[0]):
        for k in range(props.shape[1]):
            props[c, pl.ds(k, 1), :] = raw[pl.ds(c, 1), pl.ds(k * CA, CA)]


def pack_kernel(
    tops, bottoms, mates, x_ref, raw, slots, tally, to_first, to_second, crossing, props
):
    across = jnp.int32(0)
    for r in range(mates.shape[0]):
        across = jnp.where((mates[r] != r) & (mates[r] != (r ^ 1)), 1, across)
    crossing[0, 0] = across
    relay_properties(raw, props)
    width = slots.shape[1]
    for buffer in (to_first, to_second):
        buffer[5] = jnp.zeros(buffer.shape[1:], F32)
        buffer[5, pl.ds(0, 2), pl.ds(0, width)] = slots[...].astype(F32)
        buffer[5, pl.ds(2, 1), pl.ds(0, 1)] = tally[...].astype(F32)
    pack_rows(tops, bottoms, x_ref, to_first, to_second, 0, 3)
    pack_rows(tops, bottoms, props, to_first, to_second, 3, 2)


def exchange_choice(levels, mates, choice):
    own = lax.axis_index("rep")
    mate = mates[own]
    near_mate = own + 1 - 2 * lax.rem(own, 2)
    row = (1, CA)
    ratio = jnp.full(row, levels[own], F32) / jnp.full(row, levels[mate], F32)
    choice[...] = jnp.zeros_like(choice)
    choice[pl.ds(0, 1), :] = jnp.full(row, jnp.where(mate == own, 1.0, 0.0), F32)
    choice[pl.ds(1, 1), :] = jnp.full(row, jnp.where(mate == near_mate, 1.0, 0.0), F32)
    choice[pl.ds(2, 1), :] = jnp.sqrt(ratio)


def local(
    atomic_locations,
    atomic_speeds,
    atomic_properties,
    resident_tile_members,
    resident_tile_tally,
    top_edge_groups,
    bottom_edge_groups,
    boundary_tile_slots,
    boundary_tile_tally,
    spring_links,
    thermal_levels,
    exchange_mate,
):
    atoms = atomic_locations.shape[2]
    clusters = atoms // CA
    facing = top_edge_groups.shape[1]
    shape = (3, clusters, CA)
    x = atomic_locations.reshape(shape)
    v = atomic_speeds.reshape(shape)
    pairs = resident_tile_members[:, 0]
    slots = boundary_tile_slots[:, 0]
    sds = jax.ShapeDtypeStruct
    params = pltpu.CompilerParams(vmem_limit_bytes=VMEM_LIMIT)

    to_first, to_second, crossing = pl.pallas_call(
        pack_kernel,
        out_shape=(sds((6, facing, CA), F32),) * 2 + (sds((1, 1), jnp.int32),),
        in_specs=[SMEM] * 3 + [VMEM] * 4,
        out_specs=(VMEM, VMEM, SMEM),
        scratch_shapes=[pltpu.VMEM((2,) + shape[1:], F32)],
        compiler_params=pltpu.CompilerParams(vmem_limit_bytes=PACK_LIMIT),
        cost_estimate=pl.CostEstimate(
            flops=PACK_FLOPS * 1_000_000, bytes_accessed=1_000_000, transcendentals=0
        ),
        name="pack",
    )(
        top_edge_groups,
        bottom_edge_groups,
        exchange_mate,
        x,
        atomic_properties,
        slots,
        boundary_tile_tally,
    )
    first_start = swapped(to_first, "dom", 0, True)
    second_start = swapped(to_second, "dom", 1, True)

    def scratch(sources):
        return [
            pltpu.VMEM((4, clusters * ROWS, CA), F32),
            pltpu.VMEM((clusters * ROWS, CA), F32),
            pltpu.VMEM((sources, 2 * ROWS, CA), BF16),
            pltpu.VMEM((sources, 2 * ROWS, CA), BF16),
        ]

    bonds = spring_links.shape[1]
    kept = (
        sds(shape, F32),
        sds((2, 2 * CA, bonds), BF16),
        sds((2, clusters // 2, bonds), BF16),
        sds((clusters, CA, CA), F32),
    )

    def local_call(first):
        sums = (
            sds((clusters * ROWS, CA), F32),
            sds(shape, F32),
            sds((clusters, 2, 2 * ROWS, CA), BF16),
            sds((clusters, CA), F32),
        )
        rows = 3 * clusters if first else 3 * clusters // 2
        return pl.pallas_call(
            functools.partial(local_kernel, first),
            out_shape=sums + kept if first else sums,
            in_specs=[SMEM] + [VMEM] * (4 if first else 8),
            out_specs=(VMEM,) * (8 if first else 4),
            scratch_shapes=scratch(clusters)
            + [
                pltpu.VMEM((rows, 2 * CA), BF16),
                pltpu.VMEM((rows, 2 * CA), F32),
            ],
            compiler_params=params,
            cost_estimate=pl.CostEstimate(
                flops=2_000_000_000, bytes_accessed=1_000_000, transcendentals=2_000_000
            ),
            name="resident",
        )

    def edge_call(first, last, kick):
        if last:
            outs = (sds((6, clusters, CA), F32), sds((ROWS, CA), F32))
        else:
            outs = (sds(shape, F32),) * 2 + (sds((3, facing, CA), F32),) * 2
        if first:
            outs += (sds((2 * facing, CA, CA), F32),)
        return pl.pallas_call(
            functools.partial(edge_kernel, first, last, kick),
            out_shape=outs,
            in_specs=[SMEM] * (5 if last else 3) + [VMEM] * (12 if first else 13),
            out_specs=(VMEM,) * len(outs),
            scratch_shapes=scratch(2 * facing)
            + [
                pltpu.VMEM((clusters * ROWS, CA), F32),
                pltpu.VMEM((ROWS, CA), jnp.int32),
                pltpu.SMEM((ROWS, CA), jnp.int32),
                pltpu.SemaphoreType.DMA,
            ],
            compiler_params=params,
            cost_estimate=pl.CostEstimate(
                flops=1_000_000_000, bytes_accessed=1_000_000, transcendentals=2_000_000
            ),
            name="edges",
        )

    halo_ratio = ()
    first_x, second_x = first_start, second_start
    for step in range(STEPS + 1):
        if step == 0:
            acc, bonded, far, rho, props, *static = local_call(True)(
                pairs, resident_tile_tally, x, atomic_properties, spring_links
            )
        else:
            acc, bonded, far, rho = local_call(False)(
                pairs, resident_tile_tally, x, props, x_before, bonded, *static
            )
        last = step == STEPS
        kick = TIME_STEP * (0.5 if step == 0 or last else 1.0)
        results = edge_call(step == 0, last, kick)(
            top_edge_groups,
            bottom_edge_groups,
            slots,
            *((thermal_levels, exchange_mate) if last else ()),
            boundary_tile_tally,
            x,
            v,
            props,
            acc,
            bonded,
            far,
            rho,
            first_x,
            second_x,
            first_start,
            second_start,
            *halo_ratio,
        )
        if last:
            state, choice = results
        else:
            x_before = x
            x, v, to_first, to_second, *new_ratio = results
            halo_ratio = halo_ratio or new_ratio
            first_x = swapped(to_first, "dom", 0, True)
            second_x = swapped(to_second, "dom", 1, True)

    keep, near_mate, ratio = choice[0] > 0.5, choice[1] > 0.5, choice[2]
    def exchanged(state, *others):
        def part(k):
            own, *rest = [a[3 * k : 3 * k + 3] for a in (state, *others)]
            other = jnp.where(near_mate, *rest) if len(rest) == 2 else rest[0]
            return jnp.where(keep, own, other)

        return part(0), part(1) * ratio

    def with_crossing(state):
        return exchanged(state, swapped(state, "rep", 0), swapped(state, "rep", 1))

    def without_crossing(state):
        return exchanged(state, swapped(state, "rep", 0))

    new_x, new_v = lax.cond(crossing[0, 0] > 0, with_crossing, without_crossing, state)
    return new_x.reshape(3, 1, atoms), new_v.reshape(3, 1, atoms)


def solution(mesh):
    placed = (
        P(None, "rep", "dom"),
        P(None, "rep", "dom"),
        P(None, "dom"),
        P(None, "rep", "dom"),
        P("rep", "dom"),
        P("rep", "dom"),
        P("rep", "dom"),
        P(None, "rep", "dom"),
        P("rep", "dom"),
        P(None, "dom"),
        P(),
        P(),
    )
    return jax.shard_map(
        local,
        mesh=mesh,
        in_specs=placed,
        out_specs=(P(None, "rep", "dom"), P(None, "rep", "dom")),
        check_vma=False,
    )
```
